128 devices in a mesh: token: 8 (over z, x_lo), dp: 16 (over x_hi, y, core).
Axes of the slice: x: 4 (x_hi: 2, x_lo: 2; x = x_hi * 2 + x_lo), y: 4, z: 4, core: 2. Of those that a mesh axis runs over, the one named last changes fastest.
Arguments:
- inputs: bfloat16 [16384, 16, 1024], P('dp', 'token'), may hold values from -6 to 6
- cotangent: bfloat16 [16384, 16, 1024], P('dp', 'token'), may hold values from -6 to 6
- w_gate: bfloat16 [16, 1024, 768], P('token', 'dp'), may hold values from -0.1875 to 0.1875
- w_up: bfloat16 [16, 1024, 768], P('token', 'dp'), may hold values from -0.1875 to 0.1875
- w_down: bfloat16 [16, 768, 1024], P('token', 'dp'), may hold values from -0.21875 to 0.21875
Outputs:
- grad_inputs: bfloat16 [16384, 16, 1024], P('dp', 'token')
- grad_gate: bfloat16 [16, 1024, 768], P('token', 'dp')
- grad_up: bfloat16 [16, 1024, 768], P('token', 'dp')
- grad_down: bfloat16 [16, 768, 1024], P('token', 'dp')
The draws below stay inside these ranges and needn't reach their ends.
All inputs are finite; a program needn't handle non-finite values.
Results may differ from the reference program's by a relative error of at most 0.018.
Values may be sent and summed in bfloat16 or wider, within the bound.
A program may use at most 128 MiB of HBM per device.

```python
import jax
import jax.numpy as jnp
from jax import lax

D = 1024
FF = 768
TOKENS = 16
SAMPLES_DEV = 1024
SAMPLES = 16384
N_DP = 16


def shard_levels(key, extent, cuts, low, top_value):
    gain, own = 1.0, jax.random.fold_in(key, 6)
    for axis_at, blocks in cuts:
        heights = jnp.exp(jax.random.uniform(jax.random.fold_in(own, axis_at), (blocks,), jnp.float32, low / len(cuts), top_value / len(cuts)))
        gain = gain * jnp.repeat(heights, extent[axis_at] // blocks).reshape([-1 if axis == axis_at else 1 for axis in range(len(extent))])
    return gain


def normal_values(own_key, dims, width, limit, cuts=(), held_as=jnp.bfloat16):
    result = width * jax.random.normal(own_key, dims, jnp.float32)
    if cuts:
        result = result * shard_levels(own_key, dims, cuts, -0.22, 0.18)
    return jnp.clip(result, -limit, limit).astype(held_as)


def setup_inputs(seed: int = 0) -> dict:
    keys = jax.random.split(jax.random.key(seed), 6)
    return {
        "inputs": normal_values(keys[0], (SAMPLES, TOKENS, D), 1.0, 6.0, ((0, 16), (1, 8))),
        "cotangent": normal_values(keys[1], (SAMPLES, TOKENS, D), 1.0, 6.0, ((0, 16), (1, 8))),
        "w_gate": normal_values(keys[2], (TOKENS, D, FF), D ** -0.5, 0.1875, ((0, 8), (1, 16))),
        "w_up": normal_values(keys[3], (TOKENS, D, FF), D ** -0.5, 0.1875, ((0, 8), (1, 16))),
        "w_down": normal_values(keys[4], (TOKENS, FF, D), FF ** -0.5, 0.21875, ((0, 8), (1, 16))),
    }


def regroup(source):
    count = source.shape[0]
    split = source.reshape(count, TOKENS, TOKENS, D // TOKENS)
    return split.transpose(0, 2, 1, 3).reshape(count, TOKENS, D)


def backward_token(mixed_in, mixed_grad, gate_w, up_w, down_w):
    gate_pre = jnp.dot(mixed_in, gate_w, preferred_element_type=jnp.float32)
    up_pre = jnp.dot(mixed_in, up_w, preferred_element_type=jnp.float32)
    sigmoid = jax.nn.sigmoid(gate_pre)
    activated = gate_pre * sigmoid
    hidden = (activated * up_pre).astype(jnp.bfloat16)
    grad_hidden = jnp.dot(mixed_grad, down_w.T, preferred_element_type=jnp.float32)
    slope = sigmoid * (1.0 + gate_pre * (1.0 - sigmoid))
    grad_gate = (grad_hidden * up_pre * slope).astype(jnp.bfloat16)
    grad_upper = (grad_hidden * activated).astype(jnp.bfloat16)
    grad_mixed = (jnp.dot(grad_gate, gate_w.T, preferred_element_type=jnp.float32)
                  + jnp.dot(grad_upper, up_w.T, preferred_element_type=jnp.float32)).astype(jnp.bfloat16)
    return grad_mixed, grad_gate, grad_upper, hidden


def group_sum(left, right, factor):
    left_g = left.reshape(N_DP, SAMPLES_DEV, left.shape[1]).astype(jnp.float32)
    right_g = right.reshape(N_DP, SAMPLES_DEV, right.shape[1]).astype(jnp.float32)
    parts = jnp.einsum("gsa,gsb->gab", left_g, right_g).astype(jnp.bfloat16)
    parts = lax.optimization_barrier(parts)
    return (jnp.sum(parts.astype(jnp.float32), axis=0) * factor).astype(jnp.bfloat16)


def reference(inputs, cotangent, w_gate, w_up, w_down):
    factor = SAMPLES ** -0.5
    mixed_all = regroup(inputs).transpose(1, 0, 2)
    mixed_cot = regroup(cotangent).transpose(1, 0, 2)

    def one_token(items):
        mixed_in, mixed_grad, gate_w, up_w, down_w = items
        grad_mixed, grad_gate, grad_upper, hidden = backward_token(mixed_in, mixed_grad, gate_w, up_w, down_w)
        gate_sum = group_sum(mixed_in, grad_gate, factor)
        upper_sum = group_sum(mixed_in, grad_upper, factor)
        down_sum = group_sum(hidden, mixed_grad, factor)
        return grad_mixed, gate_sum, upper_sum, down_sum

    grad_mixed, grad_gate, grad_upper, grad_down = lax.map(one_token, (mixed_all, mixed_cot, w_gate, w_up, w_down))
    back = regroup(grad_mixed.transpose(1, 0, 2))
    grad_inputs = (back.astype(jnp.float32) + cotangent.astype(jnp.float32)).astype(jnp.bfloat16)
    return grad_inputs, grad_gate, grad_upper, grad_down
```

```python
import functools

import jax
import jax.numpy as jnp
from jax import lax
from jax.experimental import pallas as pl
from jax.experimental.pallas import tpu as pltpu
from jax.sharding import PartitionSpec as P

MESH = pl.DeviceIdType.MESH
BF = jnp.bfloat16
F32 = jnp.float32
LANES = 128
HALF = 64
TOKEN_DEVICES = 8
DP = 16
ROWS = 128
BLOCK = 256


def nn(a, b):
    return jnp.dot(a, b, preferred_element_type=F32)


def nt(a, b):
    return lax.dot_general(a, b, (((1,), (1,)), ((), ())), preferred_element_type=F32)


def tn(a, b):
    return lax.dot_general(a, b, (((0,), (0,)), ((), ())), preferred_element_type=F32)


def halves(a, b):
    low = jnp.concatenate([a[:, :HALF], b[:, :HALF]], axis=1)
    high = jnp.concatenate([a[:, HALF:], b[:, HALF:]], axis=1)
    return low, high


def kernel(
    factor,
    x, g, w_gate, w_up, w_down,
    out, out_gate, out_up, out_down,
    x_raw, g_raw, stage, mixed, full_gate, full_up, full_down,
    hid, g_gate, g_up, tmp,
    p_gate, p_up, p_down,
    c_gate, c_up, c_down,
    y_gate, y_up, y_down,
    s_gate, s_up, s_down,
    r_gate, r_up, r_down,
    back,
    load_sem, own_sem, wload_sem, in_send, in_recv, out_send, out_recv, own_out_sem, write_sem,
    ag_send, ag_recv, rs1_send, rs1_recv, rs2_send, rs2_recv, rs3_send, rs3_recv,
):
    samples = x.shape[0]
    me = lax.axis_index("token")
    z, xl = me // 2, me % 2
    d = lax.axis_index("dp")
    xh, y, c = d // 8, (d // 2) % 4, d % 2

    def dp_of(xh_, y_, c_):
        return xh_ * 8 + y_ * 2 + c_

    def partner(i):
        return ((z + i // 2) % 4) * 2 + (xl + i % 2) % 2

    def inverse(i):
        return ((4 - i // 2) % 4) * 2 + i % 2

    def columns(q):
        return pl.ds(pl.multiple_of(q * LANES, LANES), LANES)

    def remote(src, dst, send, recv, token_to, dp_to):
        return pltpu.make_async_remote_copy(
            src_ref=src, dst_ref=dst, send_sem=send, recv_sem=recv,
            device_id=(token_to, dp_to), device_id_type=MESH,
        )

    def load(i, which):
        src, dst = ((x, x_raw), (g, g_raw))[which]
        return pltpu.make_async_copy(
            src.at[:, :, columns(partner(i))], dst.at[i], load_sem.at[which, i]
        )

    def start_loads(i, _):
        load(i, 0).start()
        load(i, 1).start()
        return 0

    lax.fori_loop(1, TOKEN_DEVICES, start_loads, 0)
    start_loads(0, 0)
    own_weights = [
        pltpu.make_async_copy(src, dst.at[:, d], wload_sem.at[n])
        for n, (src, dst) in enumerate(
            ((w_gate, full_gate), (w_up, full_up), (w_down, full_down))
        )
    ]
    for copy in own_weights:
        copy.start()

    barrier = pltpu.get_barrier_semaphore()

    def greet(i, _):
        pl.semaphore_signal(barrier, inc=1, device_id=(partner(i), d), device_id_type=MESH)
        return 0

    lax.fori_loop(1, TOKEN_DEVICES, greet, 0)
    for to in (
        dp_of(xh, (y + 1) % 4, c),
        dp_of(xh, (y + 2) % 4, c),
        dp_of(xh, (y + 3) % 4, c),
        dp_of(1 - xh, y, c),
        dp_of(xh, y, 1 - c),
    ):
        pl.semaphore_signal(barrier, inc=1, device_id=(me, to), device_id_type=MESH)
    pl.semaphore_wait(barrier, 12)

    fulls = (full_gate, full_up, full_down)
    mine = (w_gate, w_up, w_down)
    d_x = dp_of(1 - xh, y, c)
    d_c = dp_of(xh, y, 1 - c)

    def gather(slot, shard, to, srcs=None):
        return [
            remote(
                (srcs[n] if srcs else fulls[n].at[:, shard]), fulls[n].at[:, shard],
                ag_send.at[slot, n], ag_recv.at[slot, n], me, to,
            )
            for n in range(3)
        ]

    ag_own_x = gather(0, d, d_x, mine)
    ag_own_y = [gather(dy, d, dp_of(xh, (y + dy) % 4, c), mine) for dy in (1, 2, 3)]
    ag_own_c = gather(4, d, d_c, mine)
    ag_far_y = [gather(4 + dy, d_x, dp_of(xh, (y + dy) % 4, c)) for dy in (1, 2, 3)]
    ag_far_c = gather(8, d_x, d_c)
    ag_pass_own = [gather(8 + dy, dp_of(xh, (y + 4 - dy) % 4, c), d_c) for dy in (1, 2, 3)]
    ag_pass_far = [gather(11 + dy, dp_of(1 - xh, (y + 4 - dy) % 4, c), d_c) for dy in (1, 2, 3)]

    def start_all(copies):
        for copy in copies:
            copy.start()

    start_all(ag_own_x)
    for copies in ag_own_y:
        start_all(copies)
    start_all(ag_own_c)

    def incoming(token, which, i):
        return remote(
            stage.at[token, which, i], mixed.at[token, which, :, columns(me)],
            in_send.at[token, which, i], in_recv.at[token, which, i], partner(i), d,
        )

    def shuffle(i, which):
        load(i, which).wait()
        raw = ((x_raw, g_raw)[which]).at[i].reshape(2 * samples, LANES)

        def step(k, _):
            row = pl.multiple_of(k * ROWS, ROWS)
            tmp[...] = raw[pl.ds(2 * row, 2 * ROWS), :].astype(F32)
            low, high = halves(tmp[pl.ds(0, ROWS, stride=2), :], tmp[pl.ds(1, ROWS, stride=2), :])
            stage[0, which, i, pl.ds(row, ROWS), :] = low.astype(BF)
            stage[1, which, i, pl.ds(row, ROWS), :] = high.astype(BF)
            return 0

        lax.fori_loop(0, samples // ROWS, step, 0)

    def send_in(i, _):
        shuffle(i, 0)

        @pl.when(i > 1)
        def _():
            incoming(0, 1, i - 1).start()

        shuffle(i, 1)
        incoming(0, 0, i).start()
        return 0

    lax.fori_loop(1, TOKEN_DEVICES, send_in, 0)
    shuffle(0, 0)
    incoming(0, 1, TOKEN_DEVICES - 1).start()
    shuffle(0, 1)

    def send_in_b(i, _):
        incoming(1, 0, i).start()
        incoming(1, 1, i).start()
        return 0

    lax.fori_loop(1, TOKEN_DEVICES, send_in_b, 0)
    own_in = [
        pltpu.make_async_copy(
            stage.at[token, which, 0], mixed.at[token, which, :, columns(me)], own_sem.at[token, which]
        )
        for token in range(2)
        for which in range(2)
    ]
    start_all(own_in)

    for copy in ag_own_x:
        copy.wait()
    for copies in ag_far_y:
        start_all(copies)
    start_all(ag_far_c)
    for n in range(3):
        for copy in ag_own_y[n]:
            copy.wait()
        start_all(ag_pass_own[n])
    for n in range(3):
        for copy in ag_far_y[n]:
            copy.wait()
        start_all(ag_pass_far[n])
    for copies in (ag_own_c, ag_far_c, *ag_pass_own, *ag_pass_far):
        for copy in copies:
            copy.wait()
    for copy in (*own_weights, *own_in):
        copy.wait()

    parts = (p_gate, p_up, p_down)
    cores = (c_gate, c_up, c_down)
    over_y = (y_gate, y_up, y_down)
    sums = (s_gate, s_up, s_down)
    over_x = (r_gate, r_up, r_down)
    results = (out_gate, out_up, out_down)

    def rs1(token):
        return [
            remote(
                parts[n].at[:, :, 1 - c], cores[n].at[token],
                rs1_send.at[token, n], rs1_recv.at[token, n], me, d_c,
            )
            for n in range(3)
        ]

    def rs2(token):
        return [
            remote(
                cores[n].at[token, :, (y + dy) % 4], over_y[n].at[token, dy - 1],
                rs2_send.at[token, dy - 1, n], rs2_recv.at[token, dy - 1, n],
                me, dp_of(xh, (y + dy) % 4, c),
            )
            for dy in (1, 2, 3)
            for n in range(3)
        ]

    def rs3(token):
        return [
            remote(
                sums[n].at[token], over_x[n].at[token],
                rs3_send.at[token, n], rs3_recv.at[token, n], me, d_x,
            )
            for n in range(3)
        ]

    def outgoing(token, i):
        return remote(
            stage.at[token, 0, partner(i)], back.at[token, me],
            out_send.at[token, i], out_recv.at[token, i], partner(i), d,
        )

    def own_back(token):
        return pltpu.make_async_copy(
            stage.at[token, 0, me], back.at[token, me], own_out_sem.at[token]
        )

    def wait_in(token):
        def body(i, _):
            incoming(token, 0, i).wait()
            incoming(token, 1, i).wait()
            return 0

        lax.fori_loop(1, TOKEN_DEVICES, body, 0)

    def weight(n, token):
        full = fulls[n]
        return full[token].reshape(full.shape[1] * full.shape[2], full.shape[3])

    def forward(token):
        def step(i, _):
            r = pl.ds(pl.multiple_of(i * BLOCK, BLOCK), BLOCK)
            rows = mixed[token, 0, r, :]
            gate = nn(rows, weight(0, token))
            up = nn(rows, weight(1, token))
            grad = nt(mixed[token, 1, r, :], weight(2, token))
            sig = jax.nn.sigmoid(gate)
            act = gate * sig
            hid[r, :] = (act * up).astype(BF)
            g_gate[r, :] = (grad * up * (sig * (1.0 + gate * (1.0 - sig)))).astype(BF)
            g_up[r, :] = (grad * act).astype(BF)
            return 0

        lax.fori_loop(0, samples // BLOCK, step, 0)

    def weight_terms(token):
        def step(i, _):
            left = mixed[token, 0, :, pl.ds(pl.multiple_of(i * BLOCK, BLOCK), BLOCK)]
            at = pl.ds((i % 2) * 2, 2)
            p_gate[i // 2, at] = tn(left, g_gate[...]).astype(BF).reshape(2, 2, *p_gate.shape[3:])
            p_up[i // 2, at] = tn(left, g_up[...]).astype(BF).reshape(2, 2, *p_up.shape[3:])
            return 0

        lax.fori_loop(0, 4, step, 0)
        cut = hid.shape[1] // 2

        def step_down(i, _):
            left = hid[:, pl.ds(pl.multiple_of(i * cut, LANES), cut)]
            p_down[i] = tn(left, mixed[token, 1]).astype(BF).reshape(p_down.shape[1:])
            return 0

        lax.fori_loop(0, 2, step_down, 0)

    def backward(token):
        def step(i, _):
            r = pl.ds(pl.multiple_of(i * BLOCK, BLOCK), BLOCK)
            v = (nt(g_gate[r, :], weight(0, token)) + nt(g_up[r, :], weight(1, token))).astype(BF)
            for q in range(TOKEN_DEVICES):
                stage[token, 0, q, r, :] = v[:, q * LANES : (q + 1) * LANES]
            return 0

        lax.fori_loop(0, samples // BLOCK, step, 0)

    def core_sum(token):
        def step(k, _):
            a, b = k // 4, k % 4
            for n in range(3):
                total = parts[n][a, b, c].astype(F32) + cores[n][token, a, b].astype(F32)
                cores[n][token, a, b] = total.astype(BF)
            return 0

        lax.fori_loop(0, 8, step, 0)

    def y_sum(n, token, at):
        total = cores[n][token, at, y].astype(F32)
        for dy in range(3):
            total = total + over_y[n][token, dy, at].astype(F32)
        return total

    def y_stage(token):
        for copy in rs2(token):
            copy.wait()
        for n in range(3):
            sums[n][token] = y_sum(n, token, 1 - xh).astype(BF)

    def x_stage(token):
        for copy in rs3(token):
            copy.wait()
        for n in range(3):
            total = y_sum(n, token, xh) + over_x[n][token].astype(F32)
            results[n][token] = (total * factor).astype(BF)

    def compute(token):
        forward(token)
        if token == 1:
            for copy in first_terms:
                copy.wait_send()
            y_stage(0)
            start_all(rs3(0))
        weight_terms(token)
        backward(token)
        terms = rs1(token)
        start_all(terms)

        def send_back(i, _):
            outgoing(token, i).start()
            return 0

        lax.fori_loop(1, TOKEN_DEVICES, send_back, 0)
        own_back(token).start()
        for copy in terms:
            copy.wait_recv()
        core_sum(token)
        start_all(rs2(token))
        return terms

    wait_in(0)
    first_terms = compute(0)
    wait_in(1)
    second_terms = compute(1)
    x_stage(0)

    def write(i):
        return pltpu.make_async_copy(
            x_raw.at[i], out.at[:, :, columns(partner(i))], write_sem.at[i]
        )

    def finish(i):
        q = partner(i)
        cot = g_raw.at[i].reshape(2 * samples, LANES)
        target = x_raw.at[i].reshape(2 * samples, LANES)

        def step(k, _):
            row = pl.multiple_of(k * ROWS, ROWS)
            even, odd = halves(
                back[0, q, pl.ds(row, ROWS), :].astype(F32), back[1, q, pl.ds(row, ROWS), :].astype(F32)
            )
            tmp[pl.ds(0, ROWS, stride=2), :] = even
            tmp[pl.ds(1, ROWS, stride=2), :] = odd
            both = pl.ds(2 * row, 2 * ROWS)
            target[both, :] = (tmp[...] + cot[both, :].astype(F32)).astype(BF)
            return 0

        lax.fori_loop(0, samples // ROWS, step, 0)
        write(i).start()

    own_back(0).wait()
    own_back(1).wait()
    finish(0)

    def take_back(i, _):
        outgoing(0, inverse(i)).wait_recv()
        outgoing(1, inverse(i)).wait_recv()
        finish(i)
        return 0

    lax.fori_loop(1, 5, take_back, 0)
    y_stage(1)
    start_all(rs3(1))
    lax.fori_loop(5, TOKEN_DEVICES, take_back, 0)
    x_stage(1)
    for copy in second_terms:
        copy.wait_send()

    def drain(i, _):
        outgoing(0, i).wait_send()
        outgoing(1, i).wait_send()
        write(i).wait()
        return 0

    lax.fori_loop(1, TOKEN_DEVICES, drain, 0)
    write(0).wait()


def solution(mesh):
    def per_device(inputs, cotangent, w_gate, w_up, w_down):
        samples, owned, width = inputs.shape
        up_rows, ff = w_gate.shape[1:]
        down_rows = w_down.shape[1]
        factor = float(samples * DP) ** -0.5
        anywhere = pl.BlockSpec(memory_space=pl.ANY)
        vmem = pl.BlockSpec(memory_space=pltpu.VMEM)
        dma = pltpu.SemaphoreType.DMA

        def three(*lead):
            return [
                pltpu.VMEM((*lead, up_rows, ff), BF),
                pltpu.VMEM((*lead, up_rows, ff), BF),
                pltpu.VMEM((*lead, down_rows, width), BF),
            ]

        raw = pltpu.VMEM((TOKEN_DEVICES, samples, owned, LANES), BF)
        hidden = pltpu.VMEM((samples, ff), BF)
        return pl.pallas_call(
            functools.partial(kernel, factor),
            name="mixer_backward",
            out_shape=(
                jax.ShapeDtypeStruct(inputs.shape, BF),
                jax.ShapeDtypeStruct(w_gate.shape, BF),
                jax.ShapeDtypeStruct(w_up.shape, BF),
                jax.ShapeDtypeStruct(w_down.shape, BF),
            ),
            in_specs=[anywhere] * 5,
            out_specs=(anywhere, vmem, vmem, vmem),
            scratch_shapes=[
                raw, raw,
                pltpu.VMEM((2, 2, TOKEN_DEVICES, samples, LANES), BF),
                pltpu.VMEM((2, 2, samples, width), BF),
                *three(2, DP),
                hidden, hidden, hidden,
                pltpu.VMEM((2 * ROWS, LANES), F32),
                *three(2, 4, 2),
                *three(2, 2, 4),
                *three(2, 3, 2),
                *three(2),
                *three(2),
                pltpu.VMEM((2, TOKEN_DEVICES, samples, LANES), BF),
                dma((2, TOKEN_DEVICES)), dma((2, 2)), dma((3,)),
                dma((2, 2, TOKEN_DEVICES)), dma((2, 2, TOKEN_DEVICES)),
                dma((2, TOKEN_DEVICES)), dma((2, TOKEN_DEVICES)), dma((2,)), dma((TOKEN_DEVICES,)),
                dma((15, 3)), dma((15, 3)),
                dma((2, 3)), dma((2, 3)), dma((2, 3, 3)), dma((2, 3, 3)), dma((2, 3)), dma((2, 3)),
            ],
            compiler_params=pltpu.CompilerParams(
                collective_id=0, has_side_effects=True, vmem_limit_bytes=67_000_000
            ),
        )(inputs, cotangent, w_gate, w_up, w_down)

    return jax.shard_map(
        per_device,
        mesh=mesh,
        in_specs=(
            P("dp", "token", None),
            P("dp", "token", None),
            P("token", "dp", None),
            P("token", "dp", None),
            P("token", "dp", None),
        ),
        out_specs=(
            P("dp", "token", None),
            P("token", "dp", None),
            P("token", "dp", None),
            P("token", "dp", None),
        ),
        check_vma=False,
    )
```

```python
import functools

import jax
import jax.numpy as jnp
from jax import lax
from jax.experimental import pallas as pl
from jax.experimental.pallas import tpu as pltpu
from jax.sharding import PartitionSpec as P

MESH = pl.DeviceIdType.MESH
BF = jnp.bfloat16
F32 = jnp.float32
LANES = 128
HALF = 64
TOKEN_DEVICES = 8
DP = 16
ROWS = 128
BLOCK = 256
UNROLL = 4
PIECES = 4


def nn(a, b):
    return jnp.dot(a, b, preferred_element_type=F32)


def nt(a, b):
    return lax.dot_general(a, b, (((1,), (1,)), ((), ())), preferred_element_type=F32)


def tn(a, b):
    return lax.dot_general(a, b, (((0,), (0,)), ((), ())), preferred_element_type=F32)


def halves(a, b):
    first = lax.broadcasted_iota(jnp.int32, a.shape, 1) < HALF
    turned = pltpu.roll(jnp.where(first, b, a), HALF, 1)
    return jnp.where(first, a, turned), jnp.where(first, turned, b)


def kernel(
    factor,
    x, g, w_gate, w_up, w_down,
    out, out_gate, out_up, out_down,
    x_raw, g_raw, stage, mixed, full_gate, full_up, full_down,
    hid, g_gate, g_up, tmp,
    p_gate, p_up, p_down,
    c_gate, c_up, c_down,
    y_gate, y_up, y_down,
    s_gate, s_up, s_down,
    r_gate, r_up, r_down,
    back,
    load_sem, own_sem, wload_sem, in_send, in_recv, out_send, out_recv, own_out_sem, write_sem,
    ag_send, ag_recv, rs1_send, rs1_recv, rs2_send, rs2_recv, rs3_send, rs3_recv,
):
    samples = x.shape[0]
    me = lax.axis_index("token")
    z, xl = me // 2, me % 2
    d = lax.axis_index("dp")
    xh, y, c = d // 8, (d // 2) % 4, d % 2

    def dp_of(xh_, y_, c_):
        return xh_ * 8 + y_ * 2 + c_

    def partner(i):
        return ((z + i // 2) % 4) * 2 + (xl + i % 2) % 2

    def inverse(i):
        return ((4 - i // 2) % 4) * 2 + i % 2

    def columns(q):
        return pl.ds(pl.multiple_of(q * LANES, LANES), LANES)

    def remote(src, dst, send, recv, token_to, dp_to):
        return pltpu.make_async_remote_copy(
            src_ref=src, dst_ref=dst, send_sem=send, recv_sem=recv,
            device_id=(token_to, dp_to), device_id_type=MESH,
        )

    def load(i, which):
        src, dst = ((x, x_raw), (g, g_raw))[which]
        return pltpu.make_async_copy(
            src.at[:, :, columns(partner(i))], dst.at[i], load_sem.at[which, i]
        )

    def start_loads(i, _):
        load(i, 0).start()
        load(i, 1).start()
        return 0

    lax.fori_loop(1, TOKEN_DEVICES, start_loads, 0)
    start_loads(0, 0)
    own_weights = [
        pltpu.make_async_copy(src, dst.at[:, d], wload_sem.at[n])
        for n, (src, dst) in enumerate(
            ((w_gate, full_gate), (w_up, full_up), (w_down, full_down))
        )
    ]
    for copy in own_weights:
        copy.start()

    barrier = pltpu.get_barrier_semaphore()

    def greet(i, _):
        pl.semaphore_signal(barrier, inc=1, device_id=(partner(i), d), device_id_type=MESH)
        return 0

    lax.fori_loop(1, TOKEN_DEVICES, greet, 0)
    for to in (
        dp_of(xh, (y + 1) % 4, c),
        dp_of(xh, (y + 2) % 4, c),
        dp_of(xh, (y + 3) % 4, c),
        dp_of(1 - xh, y, c),
        dp_of(xh, y, 1 - c),
    ):
        pl.semaphore_signal(barrier, inc=1, device_id=(me, to), device_id_type=MESH)
    pl.semaphore_wait(barrier, 12)

    fulls = (full_gate, full_up, full_down)
    mine = (w_gate, w_up, w_down)
    d_x = dp_of(1 - xh, y, c)
    d_c = dp_of(xh, y, 1 - c)

    def gather(slot, shard, to, srcs=None):
        return [
            remote(
                (srcs[n] if srcs else fulls[n].at[:, shard]), fulls[n].at[:, shard],
                ag_send.at[slot, n], ag_recv.at[slot, n], me, to,
            )
            for n in range(3)
        ]

    ag_own_x = gather(0, d, d_x, mine)
    ag_own_y = [gather(dy, d, dp_of(xh, (y + dy) % 4, c), mine) for dy in (1, 2, 3)]
    ag_own_c = gather(4, d, d_c, mine)
    ag_far_y = [gather(4 + dy, d_x, dp_of(xh, (y + dy) % 4, c)) for dy in (1, 2, 3)]
    ag_far_c = gather(8, d_x, d_c)
    ag_pass_own = [gather(8 + dy, dp_of(xh, (y + 4 - dy) % 4, c), d_c) for dy in (1, 2, 3)]
    ag_pass_far = [gather(11 + dy, dp_of(1 - xh, (y + 4 - dy) % 4, c), d_c) for dy in (1, 2, 3)]

    def start_all(copies):
        for copy in copies:
            copy.start()

    start_all(ag_own_x)
    for copies in ag_own_y:
        start_all(copies)
    start_all(ag_own_c)

    def incoming(token, which, i):
        return remote(
            stage.at[token, which, i], mixed.at[token, which, :, columns(me)],
            in_send.at[token, which, i], in_recv.at[token, which, i], partner(i), d,
        )

    def shuffle(i, which):
        load(i, which).wait()
        raw = ((x_raw, g_raw)[which]).at[i].reshape(2 * samples, LANES)

        def step(k, _):
            rows = [pl.multiple_of((k * UNROLL + u) * ROWS, ROWS) for u in range(UNROLL)]
            for u, row in enumerate(rows):
                tmp[u] = raw[pl.ds(2 * row, 2 * ROWS), :].astype(F32)
            for u, row in enumerate(rows):
                low, high = halves(
                    tmp[u, pl.ds(0, ROWS, stride=2), :], tmp[u, pl.ds(1, ROWS, stride=2), :]
                )
                stage[0, which, i, pl.ds(row, ROWS), :] = low.astype(BF)
                stage[1, which, i, pl.ds(row, ROWS), :] = high.astype(BF)
            return 0

        lax.fori_loop(0, samples // (ROWS * UNROLL), step, 0)

    def send_in(i, _):
        shuffle(i, 0)

        @pl.when(i > 1)
        def _():
            incoming(0, 1, i - 1).start()

        shuffle(i, 1)
        incoming(0, 0, i).start()
        return 0

    lax.fori_loop(1, TOKEN_DEVICES, send_in, 0)
    shuffle(0, 0)
    incoming(0, 1, TOKEN_DEVICES - 1).start()
    shuffle(0, 1)

    def send_in_b(i, _):
        incoming(1, 0, i).start()
        incoming(1, 1, i).start()
        return 0

    lax.fori_loop(1, TOKEN_DEVICES, send_in_b, 0)
    own_in = [
        pltpu.make_async_copy(
            stage.at[token, which, 0], mixed.at[token, which, :, columns(me)], own_sem.at[token, which]
        )
        for token in range(2)
        for which in range(2)
    ]
    start_all(own_in)

    for copy in ag_own_x:
        copy.wait()
    for copies in ag_far_y:
        start_all(copies)
    start_all(ag_far_c)
    for n in range(3):
        for copy in ag_own_y[n]:
            copy.wait()
        start_all(ag_pass_own[n])
    for n in range(3):
        for copy in ag_far_y[n]:
            copy.wait()
        start_all(ag_pass_far[n])
    for copies in (ag_own_c, ag_far_c, *ag_pass_own, *ag_pass_far):
        for copy in copies:
            copy.wait()
    for copy in (*own_weights, *own_in):
        copy.wait()

    parts = (p_gate, p_up, p_down)
    cores = (c_gate, c_up, c_down)
    over_y = (y_gate, y_up, y_down)
    sums = (s_gate, s_up, s_down)
    over_x = (r_gate, r_up, r_down)
    results = (out_gate, out_up, out_down)

    def rs1(token, n):
        return remote(
            parts[n].at[:, :, 1 - c], cores[n].at[token],
            rs1_send.at[token, n], rs1_recv.at[token, n], me, d_c,
        )

    def rs2(token, n):
        return [
            remote(
                cores[n].at[token, :, (y + dy) % 4], over_y[n].at[token, dy - 1],
                rs2_send.at[token, dy - 1, n], rs2_recv.at[token, dy - 1, n],
                me, dp_of(xh, (y + dy) % 4, c),
            )
            for dy in (1, 2, 3)
        ]

    def rs3(token, n):
        return remote(
            sums[n].at[token], over_x[n].at[token],
            rs3_send.at[token, n], rs3_recv.at[token, n], me, d_x,
        )

    def outgoing(token, i):
        return remote(
            stage.at[token, 0, partner(i)], back.at[token, me],
            out_send.at[token, i], out_recv.at[token, i], partner(i), d,
        )

    def own_back(token):
        return pltpu.make_async_copy(
            stage.at[token, 0, me], back.at[token, me], own_out_sem.at[token]
        )

    def wait_in(token):
        def body(i, _):
            incoming(token, 0, i).wait()
            incoming(token, 1, i).wait()
            return 0

        lax.fori_loop(1, TOKEN_DEVICES, body, 0)

    def weight(n, token):
        full = fulls[n]
        return full[token].reshape(full.shape[1] * full.shape[2], full.shape[3])

    def forward(token):
        def step(i, _):
            r = pl.ds(pl.multiple_of(i * BLOCK, BLOCK), BLOCK)
            rows = mixed[token, 0, r, :]
            gate = nn(rows, weight(0, token))
            up = nn(rows, weight(1, token))
            grad = nt(mixed[token, 1, r, :], weight(2, token))
            sig = jax.nn.sigmoid(gate)
            act = gate * sig
            hid[r, :] = (act * up).astype(BF)
            g_gate[r, :] = (grad * up * (sig * (1.0 + gate * (1.0 - sig)))).astype(BF)
            g_up[r, :] = (grad * act).astype(BF)
            return 0

        lax.fori_loop(0, samples // BLOCK, step, 0)

    def weight_term(n, token):
        if n == 2:
            cut = hid.shape[1] // 2

            def step_down(i, _):
                left = hid[:, pl.ds(pl.multiple_of(i * cut, LANES), cut)]
                p_down[i] = tn(left, mixed[token, 1]).astype(BF).reshape(p_down.shape[1:])
                return 0

            lax.fori_loop(0, 2, step_down, 0)
            return
        part, right = ((p_gate, g_gate), (p_up, g_up))[n]

        def step(i, _):
            left = mixed[token, 0, :, pl.ds(pl.multiple_of(i * BLOCK, BLOCK), BLOCK)]
            at = pl.ds((i % 2) * 2, 2)
            part[i // 2, at] = tn(left, right[...]).astype(BF).reshape(2, 2, *part.shape[3:])
            return 0

        lax.fori_loop(0, 4, step, 0)

    def backward(token):
        def step(i, _):
            r = pl.ds(pl.multiple_of(i * BLOCK, BLOCK), BLOCK)
            v = (nt(g_gate[r, :], weight(0, token)) + nt(g_up[r, :], weight(1, token))).astype(BF)
            for q in range(TOKEN_DEVICES):
                stage[token, 0, q, r, :] = v[:, q * LANES : (q + 1) * LANES]
            return 0

        lax.fori_loop(0, samples // BLOCK, step, 0)

    def core_stage(token, n):
        rs1(token, n).wait_recv()

        def step(k, _):
            a, b = k // 4, k % 4
            total = parts[n][a, b, c].astype(F32) + cores[n][token, a, b].astype(F32)
            cores[n][token, a, b] = total.astype(BF)
            return 0

        lax.fori_loop(0, 8, step, 0)
        start_all(rs2(token, n))

    def y_sum(n, token, at):
        total = cores[n][token, at, y].astype(F32)
        for dy in range(3):
            total = total + over_y[n][token, dy, at].astype(F32)
        return total

    def y_stage(token, n):
        for copy in rs2(token, n):
            copy.wait()
        sums[n][token] = y_sum(n, token, 1 - xh).astype(BF)
        rs3(token, n).start()

    def x_stage(token, n):
        rs3(token, n).wait()
        total = y_sum(n, token, xh) + over_x[n][token].astype(F32)
        results[n][token] = (total * factor).astype(BF)

    def compute(token):
        forward(token)
        if token == 1:
            for n in (2, 0, 1):
                rs1(0, n).wait_send()
                y_stage(0, n)
        weight_term(2, token)
        rs1(token, 2).start()
        weight_term(0, token)
        rs1(token, 0).start()
        core_stage(token, 2)
        weight_term(1, token)
        rs1(token, 1).start()
        core_stage(token, 0)
        backward(token)

        def send_back(i, _):
            outgoing(token, i).start()
            return 0

        lax.fori_loop(1, TOKEN_DEVICES, send_back, 0)
        own_back(token).start()
        core_stage(token, 1)

    wait_in(0)
    compute(0)
    wait_in(1)
    compute(1)

    def write(i):
        return pltpu.make_async_copy(
            x_raw.at[i], out.at[:, :, columns(partner(i))], write_sem.at[i]
        )

    def finish(i):
        q = partner(i)
        cot = g_raw.at[i].reshape(2 * samples, LANES)
        target = x_raw.at[i].reshape(2 * samples, LANES)

        def step(k, _):
            rows = [pl.multiple_of((k * UNROLL + u) * ROWS, ROWS) for u in range(UNROLL)]
            for u, row in enumerate(rows):
                at = pl.ds(row, ROWS)
                even, odd = halves(back[0, q, at, :].astype(F32), back[1, q, at, :].astype(F32))
                tmp[u, pl.ds(0, ROWS, stride=2), :] = even
                tmp[u, pl.ds(1, ROWS, stride=2), :] = odd
            for u, row in enumerate(rows):
                both = pl.ds(2 * row, 2 * ROWS)
                target[both, :] = (tmp[u] + cot[both, :].astype(F32)).astype(BF)
            return 0

        lax.fori_loop(0, samples // (ROWS * UNROLL), step, 0)
        write(i).start()

    def take_back(i):
        outgoing(0, inverse(i)).wait_recv()
        outgoing(1, inverse(i)).wait_recv()
        finish(i)

    own_back(0).wait()
    own_back(1).wait()
    finish(0)
    y_stage(1, 2)
    for n in range(3):
        x_stage(0, n)
    for i in (2, 4, 6):
        take_back(i)
    y_stage(1, 0)
    take_back(1)
    y_stage(1, 1)
    for i in (7, 5, 3):
        take_back(i)
    for n in (2, 0, 1):
        x_stage(1, n)
    for n in range(3):
        rs1(1, n).wait_send()

    def drain(i, _):
        outgoing(0, i).wait_send()
        outgoing(1, i).wait_send()
        write(i).wait()
        return 0

    lax.fori_loop(1, TOKEN_DEVICES, drain, 0)
    write(0).wait()


def deliver(*refs):
    sources, targets, held = refs[:4], refs[4:8], refs[8:12]
    in_sem, out_sem = refs[12:]
    rows = sources[0].shape[0] // PIECES
    routes = [
        tuple(ref.at[pl.ds(k * rows, rows)] for ref in (sources[0], held[0], targets[0]))
        for k in range(PIECES)
    ]
    routes += [(sources[n], held[n], targets[n]) for n in (1, 2, 3)]
    takes = [pltpu.make_async_copy(a, b, in_sem.at[k]) for k, (a, b, _) in enumerate(routes)]
    gives = [pltpu.make_async_copy(b, o, out_sem.at[k]) for k, (_, b, o) in enumerate(routes)]
    for take in takes:
        take.start()
    for take, give in zip(takes, gives, strict=True):
        take.wait()
        give.start()
    for give in gives:
        give.wait()


def solution(mesh):
    def per_device(inputs, cotangent, w_gate, w_up, w_down):
        samples, owned, width = inputs.shape
        up_rows, ff = w_gate.shape[1:]
        down_rows = w_down.shape[1]
        factor = float(samples * DP) ** -0.5
        anywhere = pl.BlockSpec(memory_space=pl.ANY)
        vmem = pl.BlockSpec(memory_space=pltpu.VMEM)
        dma = pltpu.SemaphoreType.DMA

        def three(*lead):
            return [
                pltpu.VMEM((*lead, up_rows, ff), BF),
                pltpu.VMEM((*lead, up_rows, ff), BF),
                pltpu.VMEM((*lead, down_rows, width), BF),
            ]

        raw = pltpu.VMEM((TOKEN_DEVICES, samples, owned, LANES), BF)
        hidden = pltpu.VMEM((samples, ff), BF)
        made = pl.pallas_call(
            functools.partial(kernel, factor),
            name="mixer_backward",
            out_shape=(
                jax.ShapeDtypeStruct(inputs.shape, BF),
                jax.ShapeDtypeStruct(w_gate.shape, BF),
                jax.ShapeDtypeStruct(w_up.shape, BF),
                jax.ShapeDtypeStruct(w_down.shape, BF),
            ),
            in_specs=[anywhere] * 5,
            out_specs=(anywhere, vmem, vmem, vmem),
            scratch_shapes=[
                raw, raw,
                pltpu.VMEM((2, 2, TOKEN_DEVICES, samples, LANES), BF),
                pltpu.VMEM((2, 2, samples, width), BF),
                *three(2, DP),
                hidden, hidden, hidden,
                pltpu.VMEM((UNROLL, 2 * ROWS, LANES), F32),
                *three(2, 4, 2),
                *three(2, 2, 4),
                *three(2, 3, 2),
                *three(2),
                *three(2),
                pltpu.VMEM((2, TOKEN_DEVICES, samples, LANES), BF),
                dma((2, TOKEN_DEVICES)), dma((2, 2)), dma((3,)),
                dma((2, 2, TOKEN_DEVICES)), dma((2, 2, TOKEN_DEVICES)),
                dma((2, TOKEN_DEVICES)), dma((2, TOKEN_DEVICES)), dma((2,)), dma((TOKEN_DEVICES,)),
                dma((15, 3)), dma((15, 3)),
                dma((2, 3)), dma((2, 3)), dma((2, 3, 3)), dma((2, 3, 3)), dma((2, 3)), dma((2, 3)),
            ],
            compiler_params=pltpu.CompilerParams(
                collective_id=0, has_side_effects=True, vmem_limit_bytes=67_000_000
            ),
        )(inputs, cotangent, w_gate, w_up, w_down)
        shapes = tuple(jax.ShapeDtypeStruct(a.shape, a.dtype) for a in made)
        return pl.pallas_call(
            deliver,
            name="deliver",
            out_shape=shapes,
            in_specs=[anywhere] * 4,
            out_specs=(anywhere,) * 4,
            scratch_shapes=[
                *(pltpu.VMEM(a.shape, a.dtype) for a in made),
                dma((PIECES + 3,)),
                dma((PIECES + 3,)),
            ],
            compiler_params=pltpu.CompilerParams(vmem_limit_bytes=67_000_000),
        )(*made)

    return jax.shard_map(
        per_device,
        mesh=mesh,
        in_specs=(
            P("dp", "token", None),
            P("dp", "token", None),
            P("token", "dp", None),
            P("token", "dp", None),
            P("token", "dp", None),
        ),
        out_specs=(
            P("dp", "token", None),
            P("token", "dp", None),
            P("token", "dp", None),
            P("token", "dp", None),
        ),
        check_vma=False,
    )
```

```python
import functools

import jax
import jax.numpy as jnp
from jax import lax
from jax.experimental import pallas as pl
from jax.experimental.pallas import tpu as pltpu
from jax.sharding import PartitionSpec as P

MESH = pl.DeviceIdType.MESH
BF = jnp.bfloat16
F32 = jnp.float32
LANES = 128
HALF = 64
TOKEN_DEVICES = 8
DP = 16
ROWS = 128
BLOCK = 256
UNROLL = 4
PIECES = 4


def nn(a, b):
    return jnp.dot(a, b, preferred_element_type=F32)


def nt(a, b):
    return lax.dot_general(a, b, (((1,), (1,)), ((), ())), preferred_element_type=F32)


def tn(a, b):
    return lax.dot_general(a, b, (((0,), (0,)), ((), ())), preferred_element_type=F32)


def halves(a, b):
    first = lax.broadcasted_iota(jnp.int32, a.shape, 1) < HALF
    turned = pltpu.roll(jnp.where(first, b, a), HALF, 1)
    return jnp.where(first, a, turned), jnp.where(first, turned, b)


def kernel(
    factor,
    x, g, w_gate, w_up, w_down,
    out, out_gate, out_up, out_down,
    x_raw, g_raw, stage, mixed, full_gate, full_up, full_down,
    hid, g_gate, g_up, tmp,
    p_gate, p_up, p_down,
    c_gate, c_up, c_down,
    y_gate, y_up, y_down,
    s_gate, s_up, s_down,
    r_gate, r_up, r_down,
    v_gate, v_up, v_down,
    u_gate, u_up, u_down,
    back,
    load_sem, own_sem, wload_sem, in_send, in_recv, out_send, out_recv, own_out_sem, write_sem,
    ag_send, ag_recv, rs1_send, rs1_recv, rs2_send, rs2_recv, rs3_send, rs3_recv,
):
    samples = x.shape[0]
    me = lax.axis_index("token")
    z, xl = me // 2, me % 2
    d = lax.axis_index("dp")
    xh, y, c = d // 8, (d // 2) % 4, d % 2

    def dp_of(xh_, y_, c_):
        return xh_ * 8 + y_ * 2 + c_

    inner = z * 2 + 1 - xl
    mate = (inner, dp_of(1 - xh, y, c))
    first, second = dp_of(0, y, c), dp_of(1, y, c)
    computed = z * 2 + (xl + xh) % 2

    def partner(i):
        return ((z + i // 2) % 4) * 2 + (xl + i % 2) % 2

    def partner_computes(i):
        return ((z + i // 2) % 4) * 2 + (xl + xh + i % 2) % 2

    def inverse(i):
        return ((4 - i // 2) % 4) * 2 + i % 2

    def columns(q):
        return pl.ds(pl.multiple_of(q * LANES, LANES), LANES)

    def remote(src, dst, send, recv, token_to, dp_to):
        return pltpu.make_async_remote_copy(
            src_ref=src, dst_ref=dst, send_sem=send, recv_sem=recv,
            device_id=(token_to, dp_to), device_id_type=MESH,
        )

    def load(i, which):
        src, dst = ((x, x_raw), (g, g_raw))[which]
        return pltpu.make_async_copy(
            src.at[:, :, columns(partner_computes(i))], dst.at[i], load_sem.at[which, i]
        )

    def start_loads(i, _):
        load(i, 0).start()
        load(i, 1).start()
        return 0

    lax.fori_loop(1, TOKEN_DEVICES, start_loads, 0)
    start_loads(0, 0)
    own_weights = [
        pltpu.make_async_copy(src, dst.at[:, d], wload_sem.at[n])
        for n, (src, dst) in enumerate(
            ((w_gate, full_gate), (w_up, full_up), (w_down, full_down))
        )
    ]

    @pl.when(xh == 0)
    def _():
        for copy in own_weights:
            copy.start()

    barrier = pltpu.get_barrier_semaphore()

    def greet(i, _):
        pl.semaphore_signal(barrier, inc=1, device_id=(partner(i), d), device_id_type=MESH)
        return 0

    lax.fori_loop(1, TOKEN_DEVICES, greet, 0)
    for to in (
        dp_of(xh, (y + 1) % 4, c),
        dp_of(xh, (y + 2) % 4, c),
        dp_of(xh, (y + 3) % 4, c),
        dp_of(xh, y, 1 - c),
    ):
        pl.semaphore_signal(barrier, inc=1, device_id=(me, to), device_id_type=MESH)
    pl.semaphore_signal(barrier, inc=1, device_id=mate, device_id_type=MESH)
    pl.semaphore_wait(barrier, 12)

    fulls = (full_gate, full_up, full_down)
    mine = (w_gate, w_up, w_down)
    relays = (v_gate, v_up, v_down)
    passing = (u_gate, u_up, u_down)
    d_c = dp_of(xh, y, 1 - c)

    def gather(token, slot, shard, to, srcs=None, dsts=None):
        return [
            remote(
                srcs[n] if srcs else fulls[n].at[token, shard],
                dsts[n] if dsts else fulls[n].at[token, shard],
                ag_send.at[token, slot, n], ag_recv.at[token, slot, n], *to,
            )
            for n in range(3)
        ]

    own = [[ref.at[token] for ref in mine] for token in range(2)]
    other_core = (me, d_c)
    first_x = [gather(token, 0, first, mate) for token in range(2)]
    second_x = (
        gather(0, 1, second, (inner, d), own[0]),
        gather(1, 1, second, (inner, d), relays),
    )
    second_mate = [gather(token, 2, second, mate) for token in range(2)]
    relay_x = gather(1, 3, second, mate, own[1], relays)

    def over_y_copies(token, far):
        shard = (first, second)[far]
        return [
            gather(token, 3 + 3 * far + dy, shard, (me, dp_of(xh, (y + dy) % 4, c))) for dy in (1, 2, 3)
        ]

    def core_copies(token, far):
        return gather(token, 10 + far, (first, second)[far], other_core)

    def pass_copies(token, far):
        return [
            gather(token, 11 + 3 * far + dy, dp_of(far, (y + 4 - dy) % 4, c), other_core)
            for dy in (1, 2, 3)
        ]

    def start_all(copies):
        for copy in copies:
            copy.start()

    def recv_all(copies):
        for copy in copies:
            copy.wait_recv()

    def send_all(copies):
        for copy in copies:
            copy.wait_send()

    def spread(token, far):
        for copies in over_y_copies(token, far):
            start_all(copies)
        start_all(core_copies(token, far))

    def pass_on(token, far):
        for arrived, onward in zip(
            over_y_copies(token, far), pass_copies(token, far), strict=True
        ):
            recv_all(arrived)
            start_all(onward)

    def gathered(token):
        for far in range(2):
            recv_all(core_copies(token, far))
            for copies in pass_copies(token, far):
                recv_all(copies)

    @pl.when(xh == 0)
    def _():
        for copy in own_weights:
            copy.wait()
        start_all(first_x[0])
        spread(0, 0)
        start_all(first_x[1])

    @pl.when(xh == 1)
    def _():
        start_all(second_x[0])
        start_all(relay_x)

    def incoming(token, which, i):
        return remote(
            stage.at[token, which, i], mixed.at[token, which, :, columns(me)],
            in_send.at[token, which, i], in_recv.at[token, which, i], partner(i), d,
        )

    def shuffle(i, which):
        load(i, which).wait()
        raw = ((x_raw, g_raw)[which]).at[i].reshape(2 * samples, LANES)

        def step(k, _):
            rows = [pl.multiple_of((k * UNROLL + u) * ROWS, ROWS) for u in range(UNROLL)]
            for u, row in enumerate(rows):
                tmp[u] = raw[pl.ds(2 * row, 2 * ROWS), :].astype(F32)
            for u, row in enumerate(rows):
                low, high = halves(
                    tmp[u, pl.ds(0, ROWS, stride=2), :], tmp[u, pl.ds(1, ROWS, stride=2), :]
                )
                stage[0, which, i, pl.ds(row, ROWS), :] = low.astype(BF)
                stage[1, which, i, pl.ds(row, ROWS), :] = high.astype(BF)
            return 0

        lax.fori_loop(0, samples // (ROWS * UNROLL), step, 0)

    def order(k):
        return jnp.where(k < 2, 1 + 2 * k, jnp.where(k < 5, 2 * k - 2, 2 * k - 5))

    def send_in(k, _):
        i = order(k)
        shuffle(i, 0)

        @pl.when(k > 0)
        def _():
            incoming(0, 1, order(k - 1)).start()

        shuffle(i, 1)
        incoming(0, 0, i).start()
        return 0

    lax.fori_loop(0, 5, send_in, 0)

    @pl.when(xh == 0)
    def _():
        recv_all(relay_x)
        start_all(second_x[1])

    @pl.when(xh == 1)
    def _():
        recv_all(first_x[0])
        spread(0, 0)
        recv_all(second_x[0])
        start_all(second_mate[0])
        spread(0, 1)

    lax.fori_loop(5, 7, send_in, 0)
    shuffle(0, 0)
    incoming(0, 1, order(6)).start()
    shuffle(0, 1)

    def send_in_b(i, _):
        incoming(1, 0, i).start()
        incoming(1, 1, i).start()
        return 0

    lax.fori_loop(1, TOKEN_DEVICES, send_in_b, 0)
    own_in = [
        pltpu.make_async_copy(
            stage.at[token, which, 0], mixed.at[token, which, :, columns(me)], own_sem.at[token, which]
        )
        for token in range(2)
        for which in range(2)
    ]
    start_all(own_in)

    @pl.when(xh == 0)
    def _():
        recv_all(second_mate[0])
        spread(0, 1)

    @pl.when(xh == 1)
    def _():
        recv_all(first_x[1])

    spread(1, 0)
    pass_on(0, 0)

    @pl.when(xh == 0)
    def _():
        recv_all(second_x[1])
        start_all(second_mate[1])
        spread(1, 1)

    pass_on(0, 1)

    @pl.when(xh == 1)
    def _():
        recv_all(second_mate[1])
        spread(1, 1)

    pass_on(1, 0)
    gathered(0)
    for copy in own_in:
        copy.wait()

    parts = (p_gate, p_up, p_down)
    cores = (c_gate, c_up, c_down)
    over_y = (y_gate, y_up, y_down)
    sums = (s_gate, s_up, s_down)
    over_x = (r_gate, r_up, r_down)
    results = (out_gate, out_up, out_down)

    def rs1(token, n):
        return remote(
            parts[n].at[:, :, 1 - c], cores[n].at[token],
            rs1_send.at[token, n], rs1_recv.at[token, n], me, d_c,
        )

    def rs2(token, n):
        return [
            remote(
                cores[n].at[token, :, (y + dy) % 4], over_y[n].at[token, dy - 1],
                rs2_send.at[token, dy - 1, n], rs2_recv.at[token, dy - 1, n],
                me, dp_of(xh, (y + dy) % 4, c),
            )
            for dy in (1, 2, 3)
        ]

    def rs3(token, n, slot):
        return remote(
            sums[n].at[token, slot], over_x[n].at[token, slot],
            rs3_send.at[token, n, slot], rs3_recv.at[token, n, slot], *mate,
        )

    def rs_relay(n):
        return remote(
            sums[n].at[0, 0], passing[n], rs3_send.at[0, n, 2], rs3_recv.at[0, n, 2], inner, d
        )

    def rs_relayed(n):
        return remote(
            passing[n], over_x[n].at[0, 0], rs3_send.at[0, n, 0], rs3_recv.at[0, n, 0], *mate
        )

    def rs_last(n):
        return remote(
            sums[n].at[1, 1], over_x[n].at[1, 1], rs3_send.at[1, n, 1], rs3_recv.at[1, n, 1], inner, d
        )

    def outgoing(token, i):
        return remote(
            stage.at[token, 0, partner(i)], back.at[token, computed],
            out_send.at[token, i], out_recv.at[token, i], partner(i), d,
        )

    def own_back(token):
        return pltpu.make_async_copy(
            stage.at[token, 0, me], back.at[token, computed], own_out_sem.at[token]
        )

    def wait_in(token):
        def body(i, _):
            incoming(token, 0, i).wait()
            incoming(token, 1, i).wait()
            return 0

        lax.fori_loop(1, TOKEN_DEVICES, body, 0)

    def weight(n, token):
        full = fulls[n]
        return full[token].reshape(full.shape[1] * full.shape[2], full.shape[3])

    def forward(token):
        def step(i, _):
            r = pl.ds(pl.multiple_of(i * BLOCK, BLOCK), BLOCK)
            rows = mixed[token, 0, r, :]
            gate = nn(rows, weight(0, token))
            up = nn(rows, weight(1, token))
            grad = nt(mixed[token, 1, r, :], weight(2, token))
            sig = jax.nn.sigmoid(gate)
            act = gate * sig
            hid[r, :] = (act * up).astype(BF)
            g_gate[r, :] = (grad * up * (sig * (1.0 + gate * (1.0 - sig)))).astype(BF)
            g_up[r, :] = (grad * act).astype(BF)
            return 0

        lax.fori_loop(0, samples // BLOCK, step, 0)

    def weight_term(n, token):
        if n == 2:
            cut = hid.shape[1] // 2

            def step_down(i, _):
                left = hid[:, pl.ds(pl.multiple_of(i * cut, LANES), cut)]
                p_down[i] = tn(left, mixed[token, 1]).astype(BF).reshape(p_down.shape[1:])
                return 0

            lax.fori_loop(0, 2, step_down, 0)
            return
        part, right = ((p_gate, g_gate), (p_up, g_up))[n]

        def step(i, _):
            left = mixed[token, 0, :, pl.ds(pl.multiple_of(i * BLOCK, BLOCK), BLOCK)]
            at = pl.ds((i % 2) * 2, 2)
            part[i // 2, at] = tn(left, right[...]).astype(BF).reshape(2, 2, *part.shape[3:])
            return 0

        lax.fori_loop(0, 4, step, 0)

    def backward(token):
        def step(i, _):
            r = pl.ds(pl.multiple_of(i * BLOCK, BLOCK), BLOCK)
            v = (nt(g_gate[r, :], weight(0, token)) + nt(g_up[r, :], weight(1, token))).astype(BF)
            for q in range(TOKEN_DEVICES):
                stage[token, 0, q, r, :] = v[:, q * LANES : (q + 1) * LANES]
            return 0

        lax.fori_loop(0, samples // BLOCK, step, 0)

    def core_stage(token, n):
        rs1(token, n).wait_recv()

        def step(k, _):
            a, b = k // 4, k % 4
            total = parts[n][a, b, c].astype(F32) + cores[n][token, a, b].astype(F32)
            cores[n][token, a, b] = total.astype(BF)
            return 0

        lax.fori_loop(0, 8, step, 0)
        start_all(rs2(token, n))

    def y_sum(n, token, at):
        total = cores[n][token, at, y].astype(F32)
        for dy in range(3):
            total = total + over_y[n][token, dy, at].astype(F32)
        return total

    def emit(n, token, total):
        results[n][token] = (total * factor).astype(BF)

    def y_stage(token, n):
        for copy in rs2(token, n):
            copy.wait()
        if token == 0:

            @pl.when(xh == 1)
            def _():
                for slot in range(2):
                    sums[n][0, slot] = y_sum(n, 0, slot).astype(BF)
                    rs3(0, n, slot).start()
        else:
            sums[n][1, 0] = y_sum(n, 1, 1 - xh).astype(BF)
            rs3(1, n, 0).start()

    def x_stage(token, n):
        if token == 0:

            @pl.when(xh == 0)
            def _():
                rs3(0, n, 0).wait_recv()
                rs3(0, n, 1).wait_recv()
                sums[n][0, 0] = (y_sum(n, 0, 1) + over_x[n][0, 1].astype(F32)).astype(BF)
                rs_relay(n).start()
                emit(n, 0, y_sum(n, 0, 0) + over_x[n][0, 0].astype(F32))
        else:
            rs3(1, n, 0).wait()
            total = y_sum(n, 1, xh) + over_x[n][1, 0].astype(F32)

            @pl.when(xh == 0)
            def _():
                emit(n, 1, total)

            @pl.when(xh == 1)
            def _():
                sums[n][1, 1] = total.astype(BF)
                rs_last(n).start()

    def relay_stage(n):
        @pl.when(xh == 0)
        def _():
            rs_relay(n).wait_recv()
            rs_relayed(n).start()

    def last_stage(token, n):
        @pl.when(xh == 1)
        def _():
            (rs_relayed(n) if token == 0 else rs_last(n)).wait_recv()
            emit(n, token, over_x[n][token, token].astype(F32))

    def compute(token):
        forward(token)
        if token == 1:
            y_stage(0, 1)
            x_stage(0, 2)
            x_stage(0, 0)
            for n in range(3):
                rs1(0, n).wait_send()
        weight_term(2, token)
        rs1(token, 2).start()
        weight_term(0, token)
        rs1(token, 0).start()
        core_stage(token, 2)
        weight_term(1, token)
        rs1(token, 1).start()
        core_stage(token, 0)
        backward(token)
        if token == 1:
            x_stage(0, 1)

        def send_back(i, _):
            outgoing(token, i).start()
            return 0

        lax.fori_loop(1, TOKEN_DEVICES, send_back, 0)
        own_back(token).start()
        core_stage(token, 1)

    wait_in(0)
    compute(0)
    pass_on(1, 1)
    gathered(1)
    y_stage(0, 2)
    y_stage(0, 0)
    wait_in(1)
    compute(1)

    def write(i):
        return pltpu.make_async_copy(
            x_raw.at[i], out.at[:, :, columns(partner_computes(i))], write_sem.at[i]
        )

    def finish(i):
        q = partner_computes(i)
        cot = g_raw.at[i].reshape(2 * samples, LANES)
        target = x_raw.at[i].reshape(2 * samples, LANES)

        def step(k, _):
            rows = [pl.multiple_of((k * UNROLL + u) * ROWS, ROWS) for u in range(UNROLL)]
            for u, row in enumerate(rows):
                at = pl.ds(row, ROWS)
                even, odd = halves(back[0, q, at, :].astype(F32), back[1, q, at, :].astype(F32))
                tmp[u, pl.ds(0, ROWS, stride=2), :] = even
                tmp[u, pl.ds(1, ROWS, stride=2), :] = odd
            for u, row in enumerate(rows):
                both = pl.ds(2 * row, 2 * ROWS)
                target[both, :] = (tmp[u] + cot[both, :].astype(F32)).astype(BF)
            return 0

        lax.fori_loop(0, samples // (ROWS * UNROLL), step, 0)
        write(i).start()

    def take_back(i):
        outgoing(0, inverse(i)).wait_recv()
        outgoing(1, inverse(i)).wait_recv()
        finish(i)

    own_back(0).wait()
    own_back(1).wait()
    finish(0)
    for n in (2, 0, 1):
        relay_stage(n)
    y_stage(1, 2)
    for i in (2, 4, 6):
        take_back(i)
    y_stage(1, 0)
    x_stage(1, 2)
    take_back(1)
    y_stage(1, 1)
    x_stage(1, 0)
    take_back(7)
    x_stage(1, 1)
    take_back(5)
    for n in (2, 0, 1):
        last_stage(0, n)
    take_back(3)
    for n in (2, 0, 1):
        last_stage(1, n)

    for token in range(2):
        for far in range(2):
            for copies in (*over_y_copies(token, far), *pass_copies(token, far)):
                send_all(copies)
            send_all(core_copies(token, far))
    for n in range(3):
        rs1(1, n).wait_send()

    @pl.when(xh == 0)
    def _():
        send_all(first_x[0])
        send_all(first_x[1])
        send_all(second_x[1])
        send_all(second_mate[1])
        for n in range(3):
            rs_relay(n).wait_send()
            rs_relayed(n).wait_send()

    @pl.when(xh == 1)
    def _():
        send_all(second_x[0])
        send_all(second_mate[0])
        send_all(relay_x)
        for n in range(3):
            rs3(0, n, 0).wait_send()
            rs3(0, n, 1).wait_send()
            rs_last(n).wait_send()

    def drain(i, _):
        outgoing(0, i).wait_send()
        outgoing(1, i).wait_send()
        write(i).wait()
        return 0

    lax.fori_loop(1, TOKEN_DEVICES, drain, 0)
    write(0).wait()


def deliver(*refs):
    sources, targets, held = refs[:4], refs[4:8], refs[8:12]
    in_sem, out_sem = refs[12:]
    rows = sources[0].shape[0] // PIECES
    routes = [
        tuple(ref.at[pl.ds(k * rows, rows)] for ref in (sources[0], held[0], targets[0]))
        for k in range(PIECES)
    ]
    routes += [(sources[n], held[n], targets[n]) for n in (1, 2, 3)]
    takes = [pltpu.make_async_copy(a, b, in_sem.at[k]) for k, (a, b, _) in enumerate(routes)]
    gives = [pltpu.make_async_copy(b, o, out_sem.at[k]) for k, (_, b, o) in enumerate(routes)]
    for take in takes:
        take.start()
    for take, give in zip(takes, gives, strict=True):
        take.wait()
        give.start()
    for give in gives:
        give.wait()


def solution(mesh):
    def per_device(inputs, cotangent, w_gate, w_up, w_down):
        samples, owned, width = inputs.shape
        up_rows, ff = w_gate.shape[1:]
        down_rows = w_down.shape[1]
        factor = float(samples * DP) ** -0.5
        anywhere = pl.BlockSpec(memory_space=pl.ANY)
        vmem = pl.BlockSpec(memory_space=pltpu.VMEM)
        dma = pltpu.SemaphoreType.DMA

        def three(*lead):
            return [
                pltpu.VMEM((*lead, up_rows, ff), BF),
                pltpu.VMEM((*lead, up_rows, ff), BF),
                pltpu.VMEM((*lead, down_rows, width), BF),
            ]

        raw = pltpu.VMEM((TOKEN_DEVICES, samples, owned, LANES), BF)
        hidden = pltpu.VMEM((samples, ff), BF)
        made = pl.pallas_call(
            functools.partial(kernel, factor),
            name="mixer_backward",
            out_shape=(
                jax.ShapeDtypeStruct(inputs.shape, BF),
                jax.ShapeDtypeStruct(w_gate.shape, BF),
                jax.ShapeDtypeStruct(w_up.shape, BF),
                jax.ShapeDtypeStruct(w_down.shape, BF),
            ),
            in_specs=[anywhere] * 5,
            out_specs=(anywhere, vmem, vmem, vmem),
            scratch_shapes=[
                raw, raw,
                pltpu.VMEM((2, 2, TOKEN_DEVICES, samples, LANES), BF),
                pltpu.VMEM((2, 2, samples, width), BF),
                *three(2, DP),
                hidden, hidden, hidden,
                pltpu.VMEM((UNROLL, 2 * ROWS, LANES), F32),
                *three(2, 4, 2),
                *three(2, 2, 4),
                *three(2, 3, 2),
                *three(2, 2),
                *three(2, 2),
                *three(),
                *three(),
                pltpu.VMEM((2, TOKEN_DEVICES, samples, LANES), BF),
                dma((2, TOKEN_DEVICES)), dma((2, 2)), dma((3,)),
                dma((2, 2, TOKEN_DEVICES)), dma((2, 2, TOKEN_DEVICES)),
                dma((2, TOKEN_DEVICES)), dma((2, TOKEN_DEVICES)), dma((2,)), dma((TOKEN_DEVICES,)),
                dma((2, 18, 3)), dma((2, 18, 3)),
                dma((2, 3)), dma((2, 3)), dma((2, 3, 3)), dma((2, 3, 3)), dma((2, 3, 3)), dma((2, 3, 3)),
            ],
            compiler_params=pltpu.CompilerParams(
                collective_id=0, has_side_effects=True, vmem_limit_bytes=67_000_000
            ),
        )(inputs, cotangent, w_gate, w_up, w_down)
        shapes = tuple(jax.ShapeDtypeStruct(a.shape, a.dtype) for a in made)
        return pl.pallas_call(
            deliver,
            name="deliver",
            out_shape=shapes,
            in_specs=[anywhere] * 4,
            out_specs=(anywhere,) * 4,
            scratch_shapes=[
                *(pltpu.VMEM(a.shape, a.dtype) for a in made),
                dma((PIECES + 3,)),
                dma((PIECES + 3,)),
            ],
            compiler_params=pltpu.CompilerParams(vmem_limit_bytes=67_000_000),
        )(*made)

    return jax.shard_map(
        per_device,
        mesh=mesh,
        in_specs=(
            P("dp", "token", None),
            P("dp", "token", None),
            P("token", "dp", None),
            P("token", "dp", None),
            P("token", "dp", None),
        ),
        out_specs=(
            P("dp", "token", None),
            P("token", "dp", None),
            P("token", "dp", None),
            P("token", "dp", None),
        ),
        check_vma=False,
    )
```

```python
import functools

import jax
import jax.numpy as jnp
from jax import lax
from jax.experimental import pallas as pl
from jax.experimental.pallas import tpu as pltpu
from jax.sharding import PartitionSpec as P

MESH = pl.DeviceIdType.MESH
BF = jnp.bfloat16
F32 = jnp.float32
LANES = 128
HALF = 64
TOKEN_DEVICES = 8
DP = 16
ROWS = 128
BLOCK = 256
UNROLL = 4


def nn(a, b):
    return jnp.dot(a, b, preferred_element_type=F32)


def nt(a, b):
    return lax.dot_general(a, b, (((1,), (1,)), ((), ())), preferred_element_type=F32)


def tn(a, b):
    return lax.dot_general(a, b, (((0,), (0,)), ((), ())), preferred_element_type=F32)


def halves(a, b):
    first = lax.broadcasted_iota(jnp.int32, a.shape, 1) < HALF
    turned = pltpu.roll(jnp.where(first, b, a), HALF, 1)
    return jnp.where(first, a, turned), jnp.where(first, turned, b)


def kernel(
    factor,
    x, g, w_gate, w_up, w_down,
    blocks, out_gate, out_up, out_down,
    g_raw, stage, mixed, full_gate, full_up, full_down,
    hid, g_gate, g_up, tmp,
    p_gate, p_up, p_down,
    c_gate, c_up, c_down,
    y_gate, y_up, y_down,
    s_gate, s_up, s_down,
    r_gate, r_up, r_down,
    v_gate, v_up, v_down,
    u_gate, u_up, u_down,
    back,
    load_sem, own_sem, wload_sem, in_send, in_recv, out_send, out_recv, own_out_sem,
    ag_send, ag_recv, rs1_send, rs1_recv, rs2_send, rs2_recv, rs3_send, rs3_recv,
):
    samples = x.shape[0]

    def wait_for(ref, sem):
        pltpu.make_async_copy(ref, ref, sem).wait()

    def wait_shards(count, sem):
        held = full_gate.at[0, pl.ds(0, count)] if count <= DP else full_gate.at[:, pl.ds(0, count // 2)]
        wait_for(held, sem)

    me = lax.axis_index("token")
    z, xl = me // 2, me % 2
    d = lax.axis_index("dp")
    xh, y, c = d // 8, (d // 2) % 4, d % 2

    def dp_of(xh_, y_, c_):
        return xh_ * 8 + y_ * 2 + c_

    inner = z * 2 + 1 - xl
    mate = (inner, dp_of(1 - xh, y, c))
    first, second = dp_of(0, y, c), dp_of(1, y, c)
    computed = z * 2 + (xl + xh) % 2

    def partner(i):
        return ((z + i // 2) % 4) * 2 + (xl + i % 2) % 2

    def partner_computes(i):
        return ((z + i // 2) % 4) * 2 + (xl + xh + i % 2) % 2

    def inverse(i):
        return ((4 - i // 2) % 4) * 2 + i % 2

    def columns(q):
        return pl.ds(pl.multiple_of(q * LANES, LANES), LANES)

    def remote(src, dst, send, recv, token_to, dp_to):
        return pltpu.make_async_remote_copy(
            src_ref=src, dst_ref=dst, send_sem=send, recv_sem=recv,
            device_id=(token_to, dp_to), device_id_type=MESH,
        )

    def load(i, which):
        q = partner_computes(i)
        src, dst = ((x, blocks.at[q]), (g, g_raw.at[i]))[which]
        return pltpu.make_async_copy(src.at[:, :, columns(q)], dst, load_sem.at[i])

    def start_loads(i, _):
        load(i, 0).start()
        load(i, 1).start()
        return 0

    lax.fori_loop(1, TOKEN_DEVICES, start_loads, 0)
    start_loads(0, 0)
    own_weights = [
        pltpu.make_async_copy(src, dst.at[:, d], wload_sem)
        for src, dst in ((w_gate, full_gate), (w_up, full_up), (w_down, full_down))
    ]

    @pl.when(xh == 0)
    def _():
        for copy in own_weights:
            copy.start()

    barrier = pltpu.get_barrier_semaphore()

    def greet(i, _):
        pl.semaphore_signal(barrier, inc=1, device_id=(partner(i), d), device_id_type=MESH)
        return 0

    lax.fori_loop(1, TOKEN_DEVICES, greet, 0)
    for to in (
        dp_of(xh, (y + 1) % 4, c),
        dp_of(xh, (y + 2) % 4, c),
        dp_of(xh, (y + 3) % 4, c),
        dp_of(xh, y, 1 - c),
    ):
        pl.semaphore_signal(barrier, inc=1, device_id=(me, to), device_id_type=MESH)
    pl.semaphore_signal(barrier, inc=1, device_id=mate, device_id_type=MESH)
    pl.semaphore_wait(barrier, 12)

    fulls = (full_gate, full_up, full_down)
    mine = (w_gate, w_up, w_down)
    relays = (v_gate, v_up, v_down)
    passing = (u_gate, u_up, u_down)
    d_c = dp_of(xh, y, 1 - c)

    def gather(token, sends, recvs, shard, to, srcs=None, dsts=None):
        return [
            remote(
                srcs[n] if srcs else fulls[n].at[token, shard],
                dsts[n] if dsts else fulls[n].at[token, shard],
                ag_send.at[sends], ag_recv.at[recvs], *to,
            )
            for n in range(3)
        ]

    own = [[ref.at[token] for ref in mine] for token in range(2)]
    other_core = (me, d_c)
    first_x = [gather(token, 8 + token, 14 + token, first, mate) for token in range(2)]
    second_x = (
        gather(0, 10, 16, second, (inner, d), own[0]),
        gather(1, 11, 17, second, (inner, d), relays),
    )
    second_mate = [gather(token, 12 + token, 18 + token, second, mate) for token in range(2)]
    relay_x = gather(1, 14, 20, second, mate, own[1], relays)

    def over_y_copies(token, far):
        shard, at = (first, second)[far], 2 * token + far
        return [
            gather(token, at, 3 * at + dy - 1, shard, (me, dp_of(xh, (y + dy) % 4, c))) for dy in (1, 2, 3)
        ]

    def core_copies(token, far):
        return gather(token, 2 * token + far, 12 + token, (first, second)[far], other_core)

    def pass_copies(token, far):
        return [
            gather(token, 4 + 2 * token + far, 12 + token, dp_of(far, (y + 4 - dy) % 4, c), other_core)
            for dy in (1, 2, 3)
        ]

    def start_all(copies):
        for copy in copies:
            copy.start()

    def arrived(slot):
        wait_shards(3, ag_recv.at[slot])

    def spread(token, far):
        for copies in over_y_copies(token, far):
            start_all(copies)
        start_all(core_copies(token, far))

    def pass_on(token, far):
        for k, onward in enumerate(pass_copies(token, far)):
            arrived(3 * (2 * token + far) + k)
            start_all(onward)

    def gathered(token):
        wait_shards(24, ag_recv.at[12 + token])

    @pl.when(xh == 0)
    def _():
        wait_shards(6, wload_sem)
        start_all(first_x[0])
        spread(0, 0)
        start_all(first_x[1])

    @pl.when(xh == 1)
    def _():
        start_all(second_x[0])
        start_all(relay_x)

    def incoming(token, which, i):
        return remote(
            stage.at[token, which, i], mixed.at[token, which, :, columns(me)],
            in_send.at[token], in_recv.at[token], partner(i), d,
        )

    def shuffle(i, which):
        if which == 0:
            wait_for(g_raw.at[pl.ds(0, 2)], load_sem.at[i])
        raw = (blocks.at[partner_computes(i)], g_raw.at[i])[which].reshape(2 * samples, LANES)

        def step(k, _):
            rows = [pl.multiple_of((k * UNROLL + u) * ROWS, ROWS) for u in range(UNROLL)]
            for u, row in enumerate(rows):
                tmp[u] = raw[pl.ds(2 * row, 2 * ROWS), :].astype(F32)
            for u, row in enumerate(rows):
                low, high = halves(
                    tmp[u, pl.ds(0, ROWS, stride=2), :], tmp[u, pl.ds(1, ROWS, stride=2), :]
                )
                stage[0, which, i, pl.ds(row, ROWS), :] = low.astype(BF)
                stage[1, which, i, pl.ds(row, ROWS), :] = high.astype(BF)
            return 0

        lax.fori_loop(0, samples // (ROWS * UNROLL), step, 0)

    def order(k):
        return jnp.where(k < 2, 1 + 2 * k, jnp.where(k < 5, 2 * k - 2, 2 * k - 5))

    def send_in(k, _):
        i = order(k)
        shuffle(i, 0)

        @pl.when(k > 0)
        def _():
            incoming(0, 1, order(k - 1)).start()

        shuffle(i, 1)
        incoming(0, 0, i).start()
        return 0

    lax.fori_loop(0, 5, send_in, 0)

    @pl.when(xh == 0)
    def _():
        arrived(20)
        start_all(second_x[1])

    @pl.when(xh == 1)
    def _():
        arrived(14)
        spread(0, 0)
        arrived(16)
        start_all(second_mate[0])
        spread(0, 1)

    lax.fori_loop(5, 7, send_in, 0)
    shuffle(0, 0)
    incoming(0, 1, order(6)).start()
    shuffle(0, 1)

    def send_in_b(i, _):
        incoming(1, 0, i).start()
        incoming(1, 1, i).start()
        return 0

    lax.fori_loop(1, TOKEN_DEVICES, send_in_b, 0)
    own_in = [
        pltpu.make_async_copy(
            stage.at[token, which, 0], mixed.at[token, which, :, columns(me)], own_sem
        )
        for token in range(2)
        for which in range(2)
    ]
    start_all(own_in)

    @pl.when(xh == 0)
    def _():
        arrived(18)
        spread(0, 1)

    @pl.when(xh == 1)
    def _():
        arrived(15)

    spread(1, 0)
    pass_on(0, 0)

    @pl.when(xh == 0)
    def _():
        arrived(17)
        start_all(second_mate[1])
        spread(1, 1)

    pass_on(0, 1)

    @pl.when(xh == 1)
    def _():
        arrived(19)
        spread(1, 1)

    pass_on(1, 0)
    gathered(0)
    wait_for(stage.at[:, :, 0], own_sem)

    parts = (p_gate, p_up, p_down)
    cores = (c_gate, c_up, c_down)
    over_y = (y_gate, y_up, y_down)
    sums = (s_gate, s_up, s_down)
    over_x = (r_gate, r_up, r_down)
    results = (out_gate, out_up, out_down)

    def rs1(token, n):
        return remote(
            parts[n].at[:, :, 1 - c], cores[n].at[token],
            rs1_send.at[token], rs1_recv.at[token, n], me, d_c,
        )

    def rs2(token, n):
        return [
            remote(
                cores[n].at[token, :, (y + dy) % 4], over_y[n].at[token, dy - 1],
                rs2_send.at[token], rs2_recv.at[token, n],
                me, dp_of(xh, (y + dy) % 4, c),
            )
            for dy in (1, 2, 3)
        ]

    def rs3(token, n, slot):
        return remote(
            sums[n].at[token, slot], over_x[n].at[token, slot],
            rs3_send.at[token], rs3_recv.at[6 * token + n], *mate,
        )

    def rs_relay(n):
        return remote(
            sums[n].at[0, 0], passing[n], rs3_send.at[0], rs3_recv.at[3 + n], inner, d
        )

    def rs_relayed(n):
        return remote(
            passing[n], over_x[n].at[0, 0], rs3_send.at[0], rs3_recv.at[n], *mate
        )

    def rs_last(n):
        return remote(
            sums[n].at[1, 1], over_x[n].at[1, 1], rs3_send.at[2], rs3_recv.at[9 + n], inner, d
        )

    def outgoing(token, i):
        return remote(
            stage.at[token, 0, partner(i)], back.at[token, computed],
            out_send.at[token], out_recv.at[i], partner(i), d,
        )

    def own_back(token):
        return pltpu.make_async_copy(
            stage.at[token, 0, me], back.at[token, computed], own_out_sem
        )

    def wait_in(token):
        sent = stage.at[token, :, pl.ds(1, TOKEN_DEVICES - 1)]
        wait_for(sent, in_send.at[token])
        wait_for(sent, in_recv.at[token])

    def weight(n, token):
        full = fulls[n]
        return full[token].reshape(full.shape[1] * full.shape[2], full.shape[3])

    def forward(token):
        def step(i, _):
            r = pl.ds(pl.multiple_of(i * BLOCK, BLOCK), BLOCK)
            rows = mixed[token, 0, r, :]
            gate = nn(rows, weight(0, token))
            up = nn(rows, weight(1, token))
            grad = nt(mixed[token, 1, r, :], weight(2, token))
            sig = jax.nn.sigmoid(gate)
            act = gate * sig
            hid[r, :] = (act * up).astype(BF)
            g_gate[r, :] = (grad * up * (sig * (1.0 + gate * (1.0 - sig)))).astype(BF)
            g_up[r, :] = (grad * act).astype(BF)
            return 0

        lax.fori_loop(0, samples // BLOCK, step, 0)

    def weight_term(n, token):
        if n == 2:
            cut = hid.shape[1] // 2

            def step_down(i, _):
                left = hid[:, pl.ds(pl.multiple_of(i * cut, LANES), cut)]
                p_down[i] = tn(left, mixed[token, 1]).astype(BF).reshape(p_down.shape[1:])
                return 0

            lax.fori_loop(0, 2, step_down, 0)
            return
        part, right = ((p_gate, g_gate), (p_up, g_up))[n]

        def step(i, _):
            left = mixed[token, 0, :, pl.ds(pl.multiple_of(i * BLOCK, BLOCK), BLOCK)]
            at = pl.ds((i % 2) * 2, 2)
            part[i // 2, at] = tn(left, right[...]).astype(BF).reshape(2, 2, *part.shape[3:])
            return 0

        lax.fori_loop(0, 4, step, 0)

    def backward(token):
        def step(i, _):
            r = pl.ds(pl.multiple_of(i * BLOCK, BLOCK), BLOCK)
            v = (nt(g_gate[r, :], weight(0, token)) + nt(g_up[r, :], weight(1, token))).astype(BF)
            for q in range(TOKEN_DEVICES):
                stage[token, 0, q, r, :] = v[:, q * LANES : (q + 1) * LANES]
            return 0

        lax.fori_loop(0, samples // BLOCK, step, 0)

    def core_stage(token, n):
        wait_shards(8, rs1_recv.at[token, n])

        def step(k, _):
            a, b = k // 4, k % 4
            total = parts[n][a, b, c].astype(F32) + cores[n][token, a, b].astype(F32)
            cores[n][token, a, b] = total.astype(BF)
            return 0

        lax.fori_loop(0, 8, step, 0)
        start_all(rs2(token, n))

    def y_sum(n, token, at):
        total = cores[n][token, at, y].astype(F32)
        for dy in range(3):
            total = total + over_y[n][token, dy, at].astype(F32)
        return total

    def emit(n, token, total):
        results[n][token] = (total * factor).astype(BF)

    def y_stage(token, n):
        wait_shards(6, rs2_recv.at[token, n])
        if token == 0:

            @pl.when(xh == 1)
            def _():
                for slot in range(2):
                    sums[n][0, slot] = y_sum(n, 0, slot).astype(BF)
                    rs3(0, n, slot).start()
        else:
            sums[n][1, 0] = y_sum(n, 1, 1 - xh).astype(BF)
            rs3(1, n, 0).start()

    def x_stage(token, n):
        if token == 0:

            @pl.when(xh == 0)
            def _():
                wait_shards(2, rs3_recv.at[n])
                sums[n][0, 0] = (y_sum(n, 0, 1) + over_x[n][0, 1].astype(F32)).astype(BF)
                rs_relay(n).start()
                emit(n, 0, y_sum(n, 0, 0) + over_x[n][0, 0].astype(F32))
        else:
            wait_shards(1, rs3_recv.at[6 + n])
            total = y_sum(n, 1, xh) + over_x[n][1, 0].astype(F32)

            @pl.when(xh == 0)
            def _():
                emit(n, 1, total)

            @pl.when(xh == 1)
            def _():
                sums[n][1, 1] = total.astype(BF)
                rs_last(n).start()

    def relay_stage(n):
        @pl.when(xh == 0)
        def _():
            wait_shards(1, rs3_recv.at[3 + n])
            rs_relayed(n).start()

    def last_stage(token, n):
        @pl.when(xh == 1)
        def _():
            wait_shards(1, rs3_recv.at[9 * token + n])
            emit(n, token, over_x[n][token, token].astype(F32))

    def compute(token):
        forward(token)
        if token == 1:
            y_stage(0, 1)
            x_stage(0, 2)
            x_stage(0, 0)
            wait_shards(24, rs1_send.at[0])
        weight_term(2, token)
        rs1(token, 2).start()
        weight_term(0, token)
        rs1(token, 0).start()
        core_stage(token, 2)
        weight_term(1, token)
        rs1(token, 1).start()
        core_stage(token, 0)
        backward(token)
        if token == 1:
            x_stage(0, 1)

        def send_back(i, _):
            outgoing(token, i).start()
            return 0

        lax.fori_loop(1, TOKEN_DEVICES, send_back, 0)
        own_back(token).start()
        core_stage(token, 1)

    wait_in(0)
    compute(0)
    pass_on(1, 1)
    gathered(1)
    y_stage(0, 2)
    y_stage(0, 0)
    wait_in(1)
    compute(1)

    def finish(i):
        q = partner_computes(i)
        cot = g_raw.at[i].reshape(2 * samples, LANES)
        target = blocks.at[q].reshape(2 * samples, LANES)

        def step(k, _):
            rows = [pl.multiple_of((k * UNROLL + u) * ROWS, ROWS) for u in range(UNROLL)]
            for u, row in enumerate(rows):
                at = pl.ds(row, ROWS)
                even, odd = halves(back[0, q, at, :].astype(F32), back[1, q, at, :].astype(F32))
                tmp[u, pl.ds(0, ROWS, stride=2), :] = even
                tmp[u, pl.ds(1, ROWS, stride=2), :] = odd
            for u, row in enumerate(rows):
                both = pl.ds(2 * row, 2 * ROWS)
                target[both, :] = (tmp[u] + cot[both, :].astype(F32)).astype(BF)
            return 0

        lax.fori_loop(0, samples // (ROWS * UNROLL), step, 0)

    def take_back(i):
        wait_for(back.at[:, 0], out_recv.at[inverse(i)])
        finish(i)

    wait_for(back.at[:, 0], own_out_sem)
    finish(0)
    for n in (2, 0, 1):
        relay_stage(n)
    y_stage(1, 2)
    for i in (2, 4, 6):
        take_back(i)
    y_stage(1, 0)
    x_stage(1, 2)
    take_back(1)
    y_stage(1, 1)
    x_stage(1, 0)
    take_back(7)
    x_stage(1, 1)
    take_back(5)
    for n in (2, 0, 1):
        last_stage(0, n)
    take_back(3)
    for n in (2, 0, 1):
        last_stage(1, n)

    for at in range(4):
        wait_shards(12, ag_send.at[at])
        wait_shards(9, ag_send.at[4 + at])
    wait_shards(24, rs1_send.at[1])
    for token in range(2):
        wait_shards(18, rs2_send.at[token])
        wait_for(stage.at[token, 0, pl.ds(1, TOKEN_DEVICES - 1)], out_send.at[token])
    wait_shards(6, rs3_send.at[0])
    wait_shards(3, rs3_send.at[1])

    @pl.when(xh == 0)
    def _():
        for at in (8, 9, 11, 13):
            wait_shards(3, ag_send.at[at])

    @pl.when(xh == 1)
    def _():
        for at in (10, 12, 14):
            wait_shards(3, ag_send.at[at])
        wait_shards(3, rs3_send.at[2])


def deliver(blocks, gate, up, down, out, out_gate, out_up, out_down, sem):
    copies = [
        pltpu.make_async_copy(
            blocks.at[q], out.at[:, :, pl.ds(q * LANES, LANES)], sem.at[q]
        )
        for q in range(TOKEN_DEVICES)
    ]
    pairs = ((gate, out_gate), (up, out_up), (down, out_down))
    copies += [pltpu.make_async_copy(a, b, sem.at[TOKEN_DEVICES + n]) for n, (a, b) in enumerate(pairs)]
    for copy in copies:
        copy.start()
    for copy in copies:
        copy.wait()


def solution(mesh):
    def per_device(inputs, cotangent, w_gate, w_up, w_down):
        samples, owned, width = inputs.shape
        up_rows, ff = w_gate.shape[1:]
        down_rows = w_down.shape[1]
        factor = float(samples * DP) ** -0.5
        anywhere = pl.BlockSpec(memory_space=pl.ANY)
        vmem = pl.BlockSpec(memory_space=pltpu.VMEM)
        dma = pltpu.SemaphoreType.DMA

        def three(*lead):
            return [
                pltpu.VMEM((*lead, up_rows, ff), BF),
                pltpu.VMEM((*lead, up_rows, ff), BF),
                pltpu.VMEM((*lead, down_rows, width), BF),
            ]

        raw = pltpu.VMEM((TOKEN_DEVICES, samples, owned, LANES), BF)
        hidden = pltpu.VMEM((samples, ff), BF)
        made = pl.pallas_call(
            functools.partial(kernel, factor),
            name="mixer_backward",
            out_shape=(
                raw,
                pltpu.VMEM(w_gate.shape, BF),
                pltpu.VMEM(w_up.shape, BF),
                pltpu.VMEM(w_down.shape, BF),
            ),
            in_specs=[anywhere] * 5,
            out_specs=(vmem,) * 4,
            scratch_shapes=[
                raw,
                pltpu.VMEM((2, 2, TOKEN_DEVICES, samples, LANES), BF),
                pltpu.VMEM((2, 2, samples, width), BF),
                *three(2, DP),
                hidden, hidden, hidden,
                pltpu.VMEM((UNROLL, 2 * ROWS, LANES), F32),
                *three(2, 4, 2),
                *three(2, 2, 4),
                *three(2, 3, 2),
                *three(2, 2),
                *three(2, 2),
                *three(),
                *three(),
                pltpu.VMEM((2, TOKEN_DEVICES, samples, LANES), BF),
                dma((TOKEN_DEVICES,)), dma(()), dma(()),
                dma((2,)), dma((2,)), dma((2,)), dma((TOKEN_DEVICES,)), dma(()),
                dma((15,)), dma((21,)),
                dma((2,)), dma((2, 3)), dma((2,)), dma((2, 3)), dma((3,)), dma((12,)),
            ],
            compiler_params=pltpu.CompilerParams(
                collective_id=0, has_side_effects=True, vmem_limit_bytes=62_000_000
            ),
        )(inputs, cotangent, w_gate, w_up, w_down)
        return pl.pallas_call(
            deliver,
            name="deliver",
            out_shape=(
                jax.ShapeDtypeStruct(inputs.shape, BF),
                jax.ShapeDtypeStruct(w_gate.shape, BF),
                jax.ShapeDtypeStruct(w_up.shape, BF),
                jax.ShapeDtypeStruct(w_down.shape, BF),
            ),
            in_specs=[vmem] * 4,
            out_specs=(anywhere,) * 4,
            scratch_shapes=[dma((TOKEN_DEVICES + 3,))],
            compiler_params=pltpu.CompilerParams(vmem_limit_bytes=1_000_000),
        )(*(pltpu.with_memory_space_constraint(a, pltpu.VMEM) for a in made))

    return jax.shard_map(
        per_device,
        mesh=mesh,
        in_specs=(
            P("dp", "token", None),
            P("dp", "token", None),
            P("token", "dp", None),
            P("token", "dp", None),
            P("token", "dp", None),
        ),
        out_specs=(
            P("dp", "token", None),
            P("token", "dp", None),
            P("token", "dp", None),
            P("token", "dp", None),
        ),
        check_vma=False,
    )
```

```python
import functools

import jax
import jax.numpy as jnp
from jax import lax
from jax.experimental import pallas as pl
from jax.experimental.pallas import tpu as pltpu
from jax.sharding import PartitionSpec as P

MESH = pl.DeviceIdType.MESH
BF = jnp.bfloat16
F32 = jnp.float32
LANES = 128
HALF = 64
TOKEN_DEVICES = 8
DP = 16
ROWS = 128
BLOCK = 256
UNROLL = 4


def nn(a, b):
    return jnp.dot(a, b, preferred_element_type=F32)


def nt(a, b):
    return lax.dot_general(a, b, (((1,), (1,)), ((), ())), preferred_element_type=F32)


def tn(a, b):
    return lax.dot_general(a, b, (((0,), (0,)), ((), ())), preferred_element_type=F32)


def halves(a, b):
    first = lax.broadcasted_iota(jnp.int32, a.shape, 1) < HALF
    turned = pltpu.roll(jnp.where(first, b, a), HALF, 1)
    return jnp.where(first, a, turned), jnp.where(first, turned, b)


def kernel(
    factor,
    x, g, w_gate, w_up, w_down,
    blocks, out_gate, out_up, out_down,
    g_raw, stage, mixed, full_gate, full_up, full_down,
    hid, g_gate, g_up, tmp,
    p_gate, p_up, p_down,
    c_gate, c_up, c_down,
    y_gate, y_up, y_down,
    s_gate, s_up, s_down,
    r_gate, r_up, r_down,
    v_gate, v_up, v_down,
    u_gate, u_up, u_down,
    back,
    load_sem, own_sem, wload_sem, in_send, in_recv, out_send, out_recv, own_out_sem,
    ag_send, ag_recv, rs1_send, rs1_recv, rs2_send, rs2_recv, rs3_send, rs3_recv,
):
    samples = x.shape[0]

    def wait_for(ref, sem):
        pltpu.make_async_copy(ref, ref, sem).wait()

    def wait_shards(count, sem):
        held = full_gate.at[0, pl.ds(0, count)] if count <= DP else full_gate.at[:, pl.ds(0, count // 2)]
        wait_for(held, sem)

    me = lax.axis_index("token")
    z, xl = me // 2, me % 2
    d = lax.axis_index("dp")
    xh, y, c = d // 8, (d // 2) % 4, d % 2

    def dp_of(xh_, y_, c_):
        return xh_ * 8 + y_ * 2 + c_

    inner = z * 2 + 1 - xl
    mate = (inner, dp_of(1 - xh, y, c))
    first, second = dp_of(0, y, c), dp_of(1, y, c)
    computed = z * 2 + (xl + xh) % 2

    def partner(i):
        return ((z + i // 2) % 4) * 2 + (xl + i % 2) % 2

    def partner_computes(i):
        return ((z + i // 2) % 4) * 2 + (xl + xh + i % 2) % 2

    def inverse(i):
        return ((4 - i // 2) % 4) * 2 + i % 2

    def columns(q):
        return pl.ds(pl.multiple_of(q * LANES, LANES), LANES)

    def remote(src, dst, send, recv, token_to, dp_to):
        return pltpu.make_async_remote_copy(
            src_ref=src, dst_ref=dst, send_sem=send, recv_sem=recv,
            device_id=(token_to, dp_to), device_id_type=MESH,
        )

    def load(i, which):
        q = partner_computes(i)
        src, dst = ((x, blocks.at[q]), (g, g_raw.at[i]))[which]
        return pltpu.make_async_copy(src.at[:, :, columns(q)], dst, load_sem.at[i])

    def start_loads(i, _):
        load(i, 0).start()
        load(i, 1).start()
        return 0

    lax.fori_loop(1, TOKEN_DEVICES, start_loads, 0)
    start_loads(0, 0)
    own_weights = [
        pltpu.make_async_copy(src, dst.at[:, d], wload_sem)
        for src, dst in ((w_gate, full_gate), (w_up, full_up), (w_down, full_down))
    ]

    @pl.when(xh == 0)
    def _():
        for copy in own_weights:
            copy.start()

    barrier = pltpu.get_barrier_semaphore()

    def greet(i, _):
        pl.semaphore_signal(barrier, inc=1, device_id=(partner(i), d), device_id_type=MESH)
        return 0

    lax.fori_loop(1, TOKEN_DEVICES, greet, 0)
    for to in (
        dp_of(xh, (y + 1) % 4, c),
        dp_of(xh, (y + 2) % 4, c),
        dp_of(xh, (y + 3) % 4, c),
        dp_of(xh, y, 1 - c),
    ):
        pl.semaphore_signal(barrier, inc=1, device_id=(me, to), device_id_type=MESH)
    pl.semaphore_signal(barrier, inc=1, device_id=mate, device_id_type=MESH)

    def incoming(token, which, i):
        return remote(
            stage.at[token, which, i], mixed.at[token, which, :, columns(me)],
            in_send.at[token], in_recv.at[token], partner(i), d,
        )

    def shuffle(i, which):
        if which == 0:
            wait_for(g_raw.at[pl.ds(0, 2)], load_sem.at[i])
        raw = (blocks.at[partner_computes(i)], g_raw.at[i])[which].reshape(2 * samples, LANES)

        def step(k, _):
            rows = [pl.multiple_of((k * UNROLL + u) * ROWS, ROWS) for u in range(UNROLL)]
            for u, row in enumerate(rows):
                tmp[u] = raw[pl.ds(2 * row, 2 * ROWS), :].astype(F32)
            for u, row in enumerate(rows):
                low, high = halves(
                    tmp[u, pl.ds(0, ROWS, stride=2), :], tmp[u, pl.ds(1, ROWS, stride=2), :]
                )
                stage[0, which, i, pl.ds(row, ROWS), :] = low.astype(BF)
                stage[1, which, i, pl.ds(row, ROWS), :] = high.astype(BF)
            return 0

        lax.fori_loop(0, samples // (ROWS * UNROLL), step, 0)

    @pl.when(xh == 0)
    def _():
        shuffle(1, 0)

    pl.semaphore_wait(barrier, 12)

    @pl.when(xh == 0)
    def _():
        incoming(0, 0, 1).start()

    fulls = (full_gate, full_up, full_down)
    mine = (w_gate, w_up, w_down)
    relays = (v_gate, v_up, v_down)
    passing = (u_gate, u_up, u_down)
    d_c = dp_of(xh, y, 1 - c)

    def gather(token, sends, recvs, shard, to, srcs=None, dsts=None):
        return [
            remote(
                srcs[n] if srcs else fulls[n].at[token, shard],
                dsts[n] if dsts else fulls[n].at[token, shard],
                ag_send.at[sends], ag_recv.at[recvs], *to,
            )
            for n in range(3)
        ]

    own = [[ref.at[token] for ref in mine] for token in range(2)]
    other_core = (me, d_c)
    first_x = [gather(token, 8 + token, 14 + token, first, mate) for token in range(2)]
    second_x = (
        gather(0, 10, 16, second, (inner, d), own[0]),
        gather(1, 11, 17, second, (inner, d), relays),
    )
    second_mate = [gather(token, 12 + token, 18 + token, second, mate) for token in range(2)]
    relay_x = gather(1, 14, 20, second, mate, own[1], relays)

    def over_y_copies(token, far):
        shard, at = (first, second)[far], 2 * token + far
        return [
            gather(token, at, 3 * at + dy - 1, shard, (me, dp_of(xh, (y + dy) % 4, c))) for dy in (1, 2, 3)
        ]

    def core_copies(token, far):
        return gather(token, 2 * token + far, 12 + token, (first, second)[far], other_core)

    def pass_copies(token, far):
        return [
            gather(token, 4 + 2 * token + far, 12 + token, dp_of(far, (y + 4 - dy) % 4, c), other_core)
            for dy in (1, 2, 3)
        ]

    def start_all(copies):
        for copy in copies:
            copy.start()

    def arrived(slot):
        wait_shards(3, ag_recv.at[slot])

    def spread(token, far):
        for copies in over_y_copies(token, far):
            start_all(copies)
        start_all(core_copies(token, far))

    def pass_on(token, far):
        for k, onward in enumerate(pass_copies(token, far)):
            arrived(3 * (2 * token + far) + k)
            start_all(onward)

    def gathered(token):
        wait_shards(24, ag_recv.at[12 + token])

    @pl.when(xh == 0)
    def _():
        wait_shards(6, wload_sem)
        start_all(first_x[0])
        spread(0, 0)
        start_all(first_x[1])

    @pl.when(xh == 1)
    def _():
        start_all(second_x[0])
        start_all(relay_x)

    def order(k):
        return jnp.where(k < 2, 1 + 2 * k, jnp.where(k < 5, 2 * k - 2, 2 * k - 5))

    def send_in(k, _):
        i = order(k)
        ahead = (k == 0) & (xh == 0)

        @pl.when(jnp.logical_not(ahead))
        def _():
            shuffle(i, 0)

        @pl.when(k > 0)
        def _():
            incoming(0, 1, order(k - 1)).start()

        shuffle(i, 1)

        @pl.when(jnp.logical_not(ahead))
        def _():
            incoming(0, 0, i).start()

        return 0

    lax.fori_loop(0, 5, send_in, 0)

    @pl.when(xh == 0)
    def _():
        arrived(20)
        start_all(second_x[1])

    @pl.when(xh == 1)
    def _():
        arrived(14)
        spread(0, 0)
        arrived(16)
        start_all(second_mate[0])
        spread(0, 1)

    lax.fori_loop(5, 7, send_in, 0)
    shuffle(0, 0)
    incoming(0, 1, order(6)).start()
    shuffle(0, 1)

    def send_in_b(i, _):
        incoming(1, 0, i).start()
        incoming(1, 1, i).start()
        return 0

    lax.fori_loop(1, TOKEN_DEVICES, send_in_b, 0)
    own_in = [
        pltpu.make_async_copy(
            stage.at[token, which, 0], mixed.at[token, which, :, columns(me)], own_sem
        )
        for token in range(2)
        for which in range(2)
    ]
    start_all(own_in)

    @pl.when(xh == 0)
    def _():
        arrived(18)
        spread(0, 1)

    @pl.when(xh == 1)
    def _():
        arrived(15)

    spread(1, 0)
    pass_on(0, 0)

    @pl.when(xh == 0)
    def _():
        arrived(17)
        start_all(second_mate[1])
        spread(1, 1)

    pass_on(0, 1)

    @pl.when(xh == 1)
    def _():
        arrived(19)
        spread(1, 1)

    pass_on(1, 0)
    gathered(0)
    wait_for(stage.at[:, :, 0], own_sem)

    parts = (p_gate, p_up, p_down)
    cores = (c_gate, c_up, c_down)
    over_y = (y_gate, y_up, y_down)
    sums = (s_gate, s_up, s_down)
    over_x = (r_gate, r_up, r_down)
    results = (out_gate, out_up, out_down)

    def rs1(token, n):
        return remote(
            parts[n].at[:, :, 1 - c], cores[n].at[token],
            rs1_send.at[token], rs1_recv.at[token, n], me, d_c,
        )

    def rs2(token, n):
        return [
            remote(
                cores[n].at[token, :, (y + dy) % 4], over_y[n].at[token, dy - 1],
                rs2_send.at[token], rs2_recv.at[token, n],
                me, dp_of(xh, (y + dy) % 4, c),
            )
            for dy in (1, 2, 3)
        ]

    def rs3(token, n, slot):
        return remote(
            sums[n].at[token, slot], over_x[n].at[token, slot],
            rs3_send.at[token], rs3_recv.at[6 * token + n], *mate,
        )

    def rs_relay(n):
        return remote(
            sums[n].at[0, 0], passing[n], rs3_send.at[0], rs3_recv.at[3 + n], inner, d
        )

    def rs_relayed(n):
        return remote(
            passing[n], over_x[n].at[0, 0], rs3_send.at[0], rs3_recv.at[n], *mate
        )

    def rs_last(n):
        return remote(
            sums[n].at[1, 1], over_x[n].at[1, 1], rs3_send.at[2], rs3_recv.at[9 + n], inner, d
        )

    def outgoing(token, i):
        return remote(
            stage.at[token, 0, partner(i)], back.at[token, computed],
            out_send.at[token], out_recv.at[i], partner(i), d,
        )

    def own_back(token):
        return pltpu.make_async_copy(
            stage.at[token, 0, me], back.at[token, computed], own_out_sem
        )

    def wait_in(token):
        sent = stage.at[token, :, pl.ds(1, TOKEN_DEVICES - 1)]
        wait_for(sent, in_send.at[token])
        wait_for(sent, in_recv.at[token])

    def weight(n, token):
        full = fulls[n]
        return full[token].reshape(full.shape[1] * full.shape[2], full.shape[3])

    def forward(token):
        def step(i, _):
            r = pl.ds(pl.multiple_of(i * BLOCK, BLOCK), BLOCK)
            rows = mixed[token, 0, r, :]
            gate = nn(rows, weight(0, token))
            up = nn(rows, weight(1, token))
            grad = nt(mixed[token, 1, r, :], weight(2, token))
            sig = jax.nn.sigmoid(gate)
            act = gate * sig
            hid[r, :] = (act * up).astype(BF)
            g_gate[r, :] = (grad * up * (sig * (1.0 + gate * (1.0 - sig)))).astype(BF)
            g_up[r, :] = (grad * act).astype(BF)
            return 0

        lax.fori_loop(0, samples // BLOCK, step, 0)

    def weight_term(n, token):
        if n == 2:
            cut = hid.shape[1] // 2

            def step_down(i, _):
                left = hid[:, pl.ds(pl.multiple_of(i * cut, LANES), cut)]
                p_down[i] = tn(left, mixed[token, 1]).astype(BF).reshape(p_down.shape[1:])
                return 0

            lax.fori_loop(0, 2, step_down, 0)
            return
        part, right = ((p_gate, g_gate), (p_up, g_up))[n]

        def step(i, _):
            left = mixed[token, 0, :, pl.ds(pl.multiple_of(i * BLOCK, BLOCK), BLOCK)]
            at = pl.ds((i % 2) * 2, 2)
            part[i // 2, at] = tn(left, right[...]).astype(BF).reshape(2, 2, *part.shape[3:])
            return 0

        lax.fori_loop(0, 4, step, 0)

    def backward(token):
        def step(i, _):
            r = pl.ds(pl.multiple_of(i * BLOCK, BLOCK), BLOCK)
            v = (nt(g_gate[r, :], weight(0, token)) + nt(g_up[r, :], weight(1, token))).astype(BF)
            for q in range(TOKEN_DEVICES):
                stage[token, 0, q, r, :] = v[:, q * LANES : (q + 1) * LANES]
            return 0

        lax.fori_loop(0, samples // BLOCK, step, 0)

    def core_stage(token, n):
        wait_shards(8, rs1_recv.at[token, n])

        def step(k, _):
            a, b = k // 4, k % 4
            total = parts[n][a, b, c].astype(F32) + cores[n][token, a, b].astype(F32)
            cores[n][token, a, b] = total.astype(BF)
            return 0

        lax.fori_loop(0, 8, step, 0)
        start_all(rs2(token, n))

    def y_sum(n, token, at):
        total = cores[n][token, at, y].astype(F32)
        for dy in range(3):
            total = total + over_y[n][token, dy, at].astype(F32)
        return total

    def emit(n, token, total):
        results[n][token] = (total * factor).astype(BF)

    def y_stage(token, n):
        wait_shards(6, rs2_recv.at[token, n])
        if token == 0:

            @pl.when(xh == 1)
            def _():
                for slot in range(2):
                    sums[n][0, slot] = y_sum(n, 0, slot).astype(BF)
                    rs3(0, n, slot).start()
        else:
            sums[n][1, 0] = y_sum(n, 1, 1 - xh).astype(BF)
            rs3(1, n, 0).start()

    def x_stage(token, n):
        if token == 0:

            @pl.when(xh == 0)
            def _():
                wait_shards(2, rs3_recv.at[n])
                sums[n][0, 0] = (y_sum(n, 0, 1) + over_x[n][0, 1].astype(F32)).astype(BF)
                rs_relay(n).start()
                emit(n, 0, y_sum(n, 0, 0) + over_x[n][0, 0].astype(F32))
        else:
            wait_shards(1, rs3_recv.at[6 + n])
            total = y_sum(n, 1, xh) + over_x[n][1, 0].astype(F32)

            @pl.when(xh == 0)
            def _():
                emit(n, 1, total)

            @pl.when(xh == 1)
            def _():
                sums[n][1, 1] = total.astype(BF)
                rs_last(n).start()

    def relay_stage(n):
        @pl.when(xh == 0)
        def _():
            wait_shards(1, rs3_recv.at[3 + n])
            rs_relayed(n).start()

    def last_stage(token, n):
        @pl.when(xh == 1)
        def _():
            wait_shards(1, rs3_recv.at[9 * token + n])
            emit(n, token, over_x[n][token, token].astype(F32))

    def compute(token):
        forward(token)
        if token == 1:
            y_stage(0, 1)
            x_stage(0, 2)
            x_stage(0, 0)
            wait_shards(24, rs1_send.at[0])
        weight_term(2, token)
        rs1(token, 2).start()
        backward(token)
        if token == 1:
            x_stage(0, 1)

        def send_back(i, _):
            outgoing(token, i).start()
            return 0

        lax.fori_loop(1, TOKEN_DEVICES, send_back, 0)
        own_back(token).start()
        core_stage(token, 2)
        weight_term(0, token)
        rs1(token, 0).start()
        weight_term(1, token)
        rs1(token, 1).start()
        core_stage(token, 0)
        core_stage(token, 1)

    wait_in(0)
    compute(0)
    pass_on(1, 1)
    gathered(1)
    y_stage(0, 2)
    y_stage(0, 0)
    wait_in(1)
    compute(1)

    def finish(i):
        q = partner_computes(i)
        cot = g_raw.at[i].reshape(2 * samples, LANES)
        target = blocks.at[q].reshape(2 * samples, LANES)

        def step(k, _):
            rows = [pl.multiple_of((k * UNROLL + u) * ROWS, ROWS) for u in range(UNROLL)]
            for u, row in enumerate(rows):
                at = pl.ds(row, ROWS)
                even, odd = halves(back[0, q, at, :].astype(F32), back[1, q, at, :].astype(F32))
                tmp[u, pl.ds(0, ROWS, stride=2), :] = even
                tmp[u, pl.ds(1, ROWS, stride=2), :] = odd
            for u, row in enumerate(rows):
                both = pl.ds(2 * row, 2 * ROWS)
                target[both, :] = (tmp[u] + cot[both, :].astype(F32)).astype(BF)
            return 0

        lax.fori_loop(0, samples // (ROWS * UNROLL), step, 0)

    def take_back(i):
        wait_for(back.at[:, 0], out_recv.at[inverse(i)])
        finish(i)

    wait_for(back.at[:, 0], own_out_sem)
    finish(0)
    for n in (2, 0, 1):
        relay_stage(n)
    y_stage(1, 2)
    for i in (2, 4, 6):
        take_back(i)
    y_stage(1, 0)
    x_stage(1, 2)
    take_back(1)
    y_stage(1, 1)
    x_stage(1, 0)
    take_back(7)
    x_stage(1, 1)
    take_back(5)
    for n in (2, 0, 1):
        last_stage(0, n)
    take_back(3)
    for n in (2, 0, 1):
        last_stage(1, n)

    for at in range(4):
        wait_shards(12, ag_send.at[at])
        wait_shards(9, ag_send.at[4 + at])
    wait_shards(24, rs1_send.at[1])
    for token in range(2):
        wait_shards(18, rs2_send.at[token])
        wait_for(stage.at[token, 0, pl.ds(1, TOKEN_DEVICES - 1)], out_send.at[token])
    wait_shards(6, rs3_send.at[0])
    wait_shards(3, rs3_send.at[1])

    @pl.when(xh == 0)
    def _():
        for at in (8, 9, 11, 13):
            wait_shards(3, ag_send.at[at])

    @pl.when(xh == 1)
    def _():
        for at in (10, 12, 14):
            wait_shards(3, ag_send.at[at])
        wait_shards(3, rs3_send.at[2])


def deliver(blocks, gate, up, down, out, out_gate, out_up, out_down, sem):
    copies = [
        pltpu.make_async_copy(
            blocks.at[q], out.at[:, :, pl.ds(q * LANES, LANES)], sem.at[q]
        )
        for q in range(TOKEN_DEVICES)
    ]
    pairs = ((gate, out_gate), (up, out_up), (down, out_down))
    copies += [pltpu.make_async_copy(a, b, sem.at[TOKEN_DEVICES + n]) for n, (a, b) in enumerate(pairs)]
    for copy in copies:
        copy.start()
    for copy in copies:
        copy.wait()


def solution(mesh):
    def per_device(inputs, cotangent, w_gate, w_up, w_down):
        samples, owned, width = inputs.shape
        up_rows, ff = w_gate.shape[1:]
        down_rows = w_down.shape[1]
        factor = float(samples * DP) ** -0.5
        anywhere = pl.BlockSpec(memory_space=pl.ANY)
        vmem = pl.BlockSpec(memory_space=pltpu.VMEM)
        dma = pltpu.SemaphoreType.DMA

        def three(*lead):
            return [
                pltpu.VMEM((*lead, up_rows, ff), BF),
                pltpu.VMEM((*lead, up_rows, ff), BF),
                pltpu.VMEM((*lead, down_rows, width), BF),
            ]

        raw = pltpu.VMEM((TOKEN_DEVICES, samples, owned, LANES), BF)
        hidden = pltpu.VMEM((samples, ff), BF)
        made = pl.pallas_call(
            functools.partial(kernel, factor),
            name="mixer_backward",
            out_shape=(
                raw,
                pltpu.VMEM(w_gate.shape, BF),
                pltpu.VMEM(w_up.shape, BF),
                pltpu.VMEM(w_down.shape, BF),
            ),
            in_specs=[anywhere] * 5,
            out_specs=(vmem,) * 4,
            scratch_shapes=[
                raw,
                pltpu.VMEM((2, 2, TOKEN_DEVICES, samples, LANES), BF),
                pltpu.VMEM((2, 2, samples, width), BF),
                *three(2, DP),
                hidden, hidden, hidden,
                pltpu.VMEM((UNROLL, 2 * ROWS, LANES), F32),
                *three(2, 4, 2),
                *three(2, 2, 4),
                *three(2, 3, 2),
                *three(2, 2),
                *three(2, 2),
                *three(),
                *three(),
                pltpu.VMEM((2, TOKEN_DEVICES, samples, LANES), BF),
                dma((TOKEN_DEVICES,)), dma(()), dma(()),
                dma((2,)), dma((2,)), dma((2,)), dma((TOKEN_DEVICES,)), dma(()),
                dma((15,)), dma((21,)),
                dma((2,)), dma((2, 3)), dma((2,)), dma((2, 3)), dma((3,)), dma((12,)),
            ],
            compiler_params=pltpu.CompilerParams(
                collective_id=0, has_side_effects=True, vmem_limit_bytes=62_000_000
            ),
        )(inputs, cotangent, w_gate, w_up, w_down)
        return pl.pallas_call(
            deliver,
            name="deliver",
            out_shape=(
                jax.ShapeDtypeStruct(inputs.shape, BF),
                jax.ShapeDtypeStruct(w_gate.shape, BF),
                jax.ShapeDtypeStruct(w_up.shape, BF),
                jax.ShapeDtypeStruct(w_down.shape, BF),
            ),
            in_specs=[vmem] * 4,
            out_specs=(anywhere,) * 4,
            scratch_shapes=[dma((TOKEN_DEVICES + 3,))],
            compiler_params=pltpu.CompilerParams(vmem_limit_bytes=1_000_000),
        )(*(pltpu.with_memory_space_constraint(a, pltpu.VMEM) for a in made))

    return jax.shard_map(
        per_device,
        mesh=mesh,
        in_specs=(
            P("dp", "token", None),
            P("dp", "token", None),
            P("token", "dp", None),
            P("token", "dp", None),
            P("token", "dp", None),
        ),
        out_specs=(
            P("dp", "token", None),
            P("token", "dp", None),
            P("token", "dp", None),
            P("token", "dp", None),
        ),
        check_vma=False,
    )
```

```python
import functools

import jax
import jax.numpy as jnp
from jax import lax
from jax.experimental import pallas as pl
from jax.experimental.pallas import tpu as pltpu
from jax.sharding import PartitionSpec as P

MESH = pl.DeviceIdType.MESH
BF = jnp.bfloat16
F32 = jnp.float32
LANES = 128
HALF = 64
TOKEN_DEVICES = 8
DP = 16
ROWS = 128
BLOCK = 256
UNROLL = 4


def nn(a, b):
    return jnp.dot(a, b, preferred_element_type=F32)


def nt(a, b):
    return lax.dot_general(a, b, (((1,), (1,)), ((), ())), preferred_element_type=F32)


def tn(a, b):
    return lax.dot_general(a, b, (((0,), (0,)), ((), ())), preferred_element_type=F32)


def halves(a, b):
    first = lax.broadcasted_iota(jnp.int32, a.shape, 1) < HALF
    turned = pltpu.roll(jnp.where(first, b, a), HALF, 1)
    return jnp.where(first, a, turned), jnp.where(first, turned, b)


def kernel(
    factor,
    x, g, w_gate, w_up, w_down,
    blocks, out_gate, out_up, out_down,
    g_raw, stage, mixed, full_gate, full_up, full_down,
    hid, g_gate, g_up, tmp,
    p_gate, p_up, p_down,
    c_gate, c_up, c_down,
    y_gate, y_up, y_down,
    s_gate, s_up, s_down,
    r_gate, r_up, r_down,
    v_gate, v_up, v_down,
    u_gate, u_up, u_down,
    back,
    load_sem, own_sem, wload_sem, in_send, in_recv, out_send, out_recv, own_out_sem,
    ag_send, ag_recv, rs1_send, rs1_recv, rs2_send, rs2_recv, rs3_send, rs3_recv,
):
    samples = x.shape[0]

    def wait_for(ref, sem):
        pltpu.make_async_copy(ref, ref, sem).wait()

    def wait_shards(count, sem):
        held = full_gate.at[0, pl.ds(0, count)] if count <= DP else full_gate.at[:, pl.ds(0, count // 2)]
        wait_for(held, sem)

    me = lax.axis_index("token")
    z, xl = me // 2, me % 2
    d = lax.axis_index("dp")
    xh, y, c = d // 8, (d // 2) % 4, d % 2

    def dp_of(xh_, y_, c_):
        return xh_ * 8 + y_ * 2 + c_

    inner = z * 2 + 1 - xl
    mate = (inner, dp_of(1 - xh, y, c))
    first, second = dp_of(0, y, c), dp_of(1, y, c)
    computed = z * 2 + (xl + xh) % 2

    def partner(i):
        return ((z + i // 2) % 4) * 2 + (xl + i % 2) % 2

    def partner_computes(i):
        return ((z + i // 2) % 4) * 2 + (xl + xh + i % 2) % 2

    def inverse(i):
        return ((4 - i // 2) % 4) * 2 + i % 2

    def columns(q):
        return pl.ds(pl.multiple_of(q * LANES, LANES), LANES)

    def remote(src, dst, send, recv, token_to, dp_to):
        return pltpu.make_async_remote_copy(
            src_ref=src, dst_ref=dst, send_sem=send, recv_sem=recv,
            device_id=(token_to, dp_to), device_id_type=MESH,
        )

    def load(i, which):
        q = partner_computes(i)
        src, dst = ((x, blocks.at[q]), (g, g_raw.at[i]))[which]
        return pltpu.make_async_copy(src.at[:, :, columns(q)], dst, load_sem.at[i])

    def start_loads(i, _):
        load(i, 0).start()
        load(i, 1).start()
        return 0

    lax.fori_loop(1, TOKEN_DEVICES, start_loads, 0)
    start_loads(0, 0)
    own_weights = [
        pltpu.make_async_copy(src, dst.at[:, d], wload_sem)
        for src, dst in ((w_gate, full_gate), (w_up, full_up), (w_down, full_down))
    ]

    @pl.when(xh == 0)
    def _():
        for copy in own_weights:
            copy.start()

    barrier = pltpu.get_barrier_semaphore()

    def greet(i, _):
        pl.semaphore_signal(barrier, inc=1, device_id=(partner(i), d), device_id_type=MESH)
        return 0

    lax.fori_loop(1, TOKEN_DEVICES, greet, 0)
    for to in (
        dp_of(xh, (y + 1) % 4, c),
        dp_of(xh, (y + 2) % 4, c),
        dp_of(xh, (y + 3) % 4, c),
        dp_of(xh, y, 1 - c),
    ):
        pl.semaphore_signal(barrier, inc=1, device_id=(me, to), device_id_type=MESH)
    pl.semaphore_signal(barrier, inc=1, device_id=mate, device_id_type=MESH)

    def incoming(token, which, i):
        return remote(
            stage.at[token, which, i], mixed.at[token, which, :, columns(me)],
            in_send.at[token], in_recv.at[token], partner(i), d,
        )

    def shuffle(i, which):
        if which == 0:
            wait_for(g_raw.at[pl.ds(0, 2)], load_sem.at[i])
        raw = (blocks.at[partner_computes(i)], g_raw.at[i])[which].reshape(2 * samples, LANES)

        def step(k, _):
            rows = [pl.multiple_of((k * UNROLL + u) * ROWS, ROWS) for u in range(UNROLL)]
            for u, row in enumerate(rows):
                tmp[u] = raw[pl.ds(2 * row, 2 * ROWS), :].astype(F32)
            for u, row in enumerate(rows):
                low, high = halves(
                    tmp[u, pl.ds(0, ROWS, stride=2), :], tmp[u, pl.ds(1, ROWS, stride=2), :]
                )
                stage[0, which, i, pl.ds(row, ROWS), :] = low.astype(BF)
                stage[1, which, i, pl.ds(row, ROWS), :] = high.astype(BF)
            return 0

        lax.fori_loop(0, samples // (ROWS * UNROLL), step, 0)

    @pl.when(xh == 0)
    def _():
        shuffle(1, 0)

    pl.semaphore_wait(barrier, 12)

    @pl.when(xh == 0)
    def _():
        incoming(0, 0, 1).start()

    fulls = (full_gate, full_up, full_down)
    mine = (w_gate, w_up, w_down)
    relays = (v_gate, v_up, v_down)
    passing = (u_gate, u_up, u_down)
    d_c = dp_of(xh, y, 1 - c)

    def gather(token, sends, recvs, shard, to, srcs=None, dsts=None):
        return [
            remote(
                srcs[n] if srcs else fulls[n].at[token, shard],
                dsts[n] if dsts else fulls[n].at[token, shard],
                ag_send.at[sends], ag_recv.at[recvs], *to,
            )
            for n in range(3)
        ]

    own = [[ref.at[token] for ref in mine] for token in range(2)]
    other_core = (me, d_c)
    first_x = [gather(token, 8 + token, 14 + token, first, mate) for token in range(2)]
    second_x = (
        gather(0, 10, 16, second, (inner, d), own[0]),
        gather(1, 11, 17, second, (inner, d), relays),
    )
    second_mate = [gather(token, 12 + token, 18 + token, second, mate) for token in range(2)]
    relay_x = gather(1, 14, 20, second, mate, own[1], relays)

    def over_y_copies(token, far):
        shard, at = (first, second)[far], 2 * token + far
        return [
            gather(token, at, 3 * at + dy - 1, shard, (me, dp_of(xh, (y + dy) % 4, c))) for dy in (1, 2, 3)
        ]

    def core_copies(token, far):
        return gather(token, 2 * token + far, 12 + token, (first, second)[far], other_core)

    def pass_copies(token, far):
        return [
            gather(token, 4 + 2 * token + far, 12 + token, dp_of(far, (y + 4 - dy) % 4, c), other_core)
            for dy in (1, 2, 3)
        ]

    def start_all(copies):
        for copy in copies:
            copy.start()

    def arrived(slot):
        wait_shards(3, ag_recv.at[slot])

    def spread(token, far):
        for copies in over_y_copies(token, far):
            start_all(copies)
        start_all(core_copies(token, far))

    def pass_on(token, far):
        for k, onward in enumerate(pass_copies(token, far)):
            arrived(3 * (2 * token + far) + k)
            start_all(onward)

    def gathered(token):
        wait_shards(24, ag_recv.at[12 + token])

    @pl.when(xh == 0)
    def _():
        wait_shards(6, wload_sem)
        start_all(first_x[0])
        spread(0, 0)
        start_all(first_x[1])

    @pl.when(xh == 1)
    def _():
        start_all(second_x[0])
        start_all(relay_x)

    def order(k):
        return jnp.where(k < 2, 1 + 2 * k, jnp.where(k < 5, 2 * k - 2, 2 * k - 5))

    def send_in(k, _):
        i = order(k)
        ahead = (k == 0) & (xh == 0)

        @pl.when(jnp.logical_not(ahead))
        def _():
            shuffle(i, 0)

        @pl.when(k > 0)
        def _():
            incoming(0, 1, order(k - 1)).start()

        shuffle(i, 1)

        @pl.when(jnp.logical_not(ahead))
        def _():
            incoming(0, 0, i).start()

        return 0

    lax.fori_loop(0, 5, send_in, 0)

    @pl.when(xh == 0)
    def _():
        arrived(20)
        start_all(second_x[1])

    @pl.when(xh == 1)
    def _():
        arrived(14)
        spread(0, 0)
        arrived(16)
        start_all(second_mate[0])
        spread(0, 1)

    lax.fori_loop(5, 7, send_in, 0)
    shuffle(0, 0)
    incoming(0, 1, order(6)).start()
    shuffle(0, 1)

    def send_in_b(i, _):
        incoming(1, 0, i).start()
        incoming(1, 1, i).start()
        return 0

    lax.fori_loop(1, TOKEN_DEVICES, send_in_b, 0)
    own_in = [
        pltpu.make_async_copy(
            stage.at[token, which, 0], mixed.at[token, which, :, columns(me)], own_sem
        )
        for token in range(2)
        for which in range(2)
    ]
    start_all(own_in)

    @pl.when(xh == 0)
    def _():
        arrived(18)
        spread(0, 1)

    @pl.when(xh == 1)
    def _():
        arrived(15)

    spread(1, 0)
    pass_on(0, 0)

    @pl.when(xh == 0)
    def _():
        arrived(17)
        start_all(second_mate[1])
        spread(1, 1)

    pass_on(0, 1)

    @pl.when(xh == 1)
    def _():
        arrived(19)
        spread(1, 1)

    pass_on(1, 0)
    gathered(0)
    wait_for(stage.at[:, :, 0], own_sem)

    parts = (p_gate, p_up, p_down)
    cores = (c_gate, c_up, c_down)
    over_y = (y_gate, y_up, y_down)
    sums = (s_gate, s_up, s_down)
    over_x = (r_gate, r_up, r_down)
    results = (out_gate, out_up, out_down)

    def rs1(token, n):
        return remote(
            parts[n].at[:, :, 1 - c], cores[n].at[token],
            rs1_send.at[token], rs1_recv.at[token, n], me, d_c,
        )

    def rs2(token, n):
        return [
            remote(
                cores[n].at[token, :, (y + dy) % 4], over_y[n].at[token, dy - 1],
                rs2_send.at[token], rs2_recv.at[token, n],
                me, dp_of(xh, (y + dy) % 4, c),
            )
            for dy in (1, 2, 3)
        ]

    def rs3(token, n, slot):
        return remote(
            sums[n].at[token, slot], over_x[n].at[token, slot],
            rs3_send.at[token], rs3_recv.at[6 * token + n], *mate,
        )

    def rs_relay(n):
        return remote(
            sums[n].at[0, 0], passing[n], rs3_send.at[0], rs3_recv.at[3 + n], inner, d
        )

    def rs_relayed(n):
        return remote(
            passing[n], over_x[n].at[0, 0], rs3_send.at[0], rs3_recv.at[n], *mate
        )

    def rs_last(n):
        return remote(
            sums[n].at[1, 1], over_x[n].at[1, 1], rs3_send.at[2], rs3_recv.at[9 + n], inner, d
        )

    def outgoing(token, i):
        return remote(
            stage.at[token, 0, partner(i)], back.at[token, computed],
            out_send.at[token], out_recv.at[i], partner(i), d,
        )

    def own_back(token):
        return pltpu.make_async_copy(
            stage.at[token, 0, me], back.at[token, computed], own_out_sem
        )

    def wait_in(token):
        sent = stage.at[token, :, pl.ds(1, TOKEN_DEVICES - 1)]
        wait_for(sent, in_send.at[token])
        wait_for(sent, in_recv.at[token])

    def weight(n, token):
        full = fulls[n]
        return full[token].reshape(full.shape[1] * full.shape[2], full.shape[3])

    def forward(token):
        def step(i, _):
            r = pl.ds(pl.multiple_of(i * BLOCK, BLOCK), BLOCK)
            rows = mixed[token, 0, r, :]
            gate = nn(rows, weight(0, token))
            up = nn(rows, weight(1, token))
            grad = nt(mixed[token, 1, r, :], weight(2, token))
            sig = jax.nn.sigmoid(gate)
            act = gate * sig
            hid[r, :] = (act * up).astype(BF)
            g_gate[r, :] = (grad * up * (sig * (1.0 + gate * (1.0 - sig)))).astype(BF)
            g_up[r, :] = (grad * act).astype(BF)
            return 0

        lax.fori_loop(0, samples // BLOCK, step, 0)

    def weight_term(n, token):
        if n == 2:
            cut = hid.shape[1] // 2

            def step_down(i, _):
                left = hid[:, pl.ds(pl.multiple_of(i * cut, LANES), cut)]
                p_down[i] = tn(left, mixed[token, 1]).astype(BF).reshape(p_down.shape[1:])
                return 0

            lax.fori_loop(0, 2, step_down, 0)
            return
        part, right = ((p_gate, g_gate), (p_up, g_up))[n]

        def step(i, _):
            left = mixed[token, 0, :, pl.ds(pl.multiple_of(i * BLOCK, BLOCK), BLOCK)]
            at = pl.ds((i % 2) * 2, 2)
            part[i // 2, at] = tn(left, right[...]).astype(BF).reshape(2, 2, *part.shape[3:])
            return 0

        lax.fori_loop(0, 4, step, 0)

    def backward(token):
        def step(i, _):
            r = pl.ds(pl.multiple_of(i * 2 * BLOCK, 2 * BLOCK), 2 * BLOCK)
            v = (nt(g_gate[r, :], weight(0, token)) + nt(g_up[r, :], weight(1, token))).astype(BF)
            for q in range(TOKEN_DEVICES):
                stage[token, 0, q, r, :] = v[:, q * LANES : (q + 1) * LANES]
            return 0

        lax.fori_loop(0, samples // (2 * BLOCK), step, 0)

    def core_stage(token, n):
        wait_shards(8, rs1_recv.at[token, n])

        def step(k, _):
            a, b = k // 4, k % 4
            total = parts[n][a, b, c].astype(F32) + cores[n][token, a, b].astype(F32)
            cores[n][token, a, b] = total.astype(BF)
            return 0

        lax.fori_loop(0, 8, step, 0)
        start_all(rs2(token, n))

    def y_sum(n, token, at):
        total = cores[n][token, at, y].astype(F32)
        for dy in range(3):
            total = total + over_y[n][token, dy, at].astype(F32)
        return total

    def emit(n, token, total):
        results[n][token] = (total * factor).astype(BF)

    def y_stage(token, n):
        wait_shards(6, rs2_recv.at[token, n])
        if token == 0:

            @pl.when(xh == 1)
            def _():
                for slot in range(2):
                    sums[n][0, slot] = y_sum(n, 0, slot).astype(BF)
                    rs3(0, n, slot).start()
        else:
            sums[n][1, 0] = y_sum(n, 1, 1 - xh).astype(BF)
            rs3(1, n, 0).start()

    def x_stage(token, n):
        if token == 0:

            @pl.when(xh == 0)
            def _():
                wait_shards(2, rs3_recv.at[n])
                sums[n][0, 0] = (y_sum(n, 0, 1) + over_x[n][0, 1].astype(F32)).astype(BF)
                rs_relay(n).start()
                emit(n, 0, y_sum(n, 0, 0) + over_x[n][0, 0].astype(F32))
        else:
            wait_shards(1, rs3_recv.at[6 + n])
            total = y_sum(n, 1, xh) + over_x[n][1, 0].astype(F32)

            @pl.when(xh == 0)
            def _():
                emit(n, 1, total)

            @pl.when(xh == 1)
            def _():
                sums[n][1, 1] = total.astype(BF)
                rs_last(n).start()

    def relay_stage(n):
        @pl.when(xh == 0)
        def _():
            wait_shards(1, rs3_recv.at[3 + n])
            rs_relayed(n).start()

    def last_stage(token, n):
        @pl.when(xh == 1)
        def _():
            wait_shards(1, rs3_recv.at[9 * token + n])
            emit(n, token, over_x[n][token, token].astype(F32))

    def compute(token):
        forward(token)
        if token == 1:
            y_stage(0, 1)
            x_stage(0, 2)
            x_stage(0, 0)
            wait_shards(24, rs1_send.at[0])
        weight_term(2, token)
        rs1(token, 2).start()
        backward(token)
        if token == 1:
            x_stage(0, 1)

        def send_back(i, _):
            outgoing(token, i).start()
            return 0

        lax.fori_loop(1, TOKEN_DEVICES, send_back, 0)
        own_back(token).start()
        core_stage(token, 2)
        weight_term(0, token)
        rs1(token, 0).start()
        weight_term(1, token)
        rs1(token, 1).start()
        core_stage(token, 0)
        core_stage(token, 1)

    wait_in(0)
    compute(0)
    pass_on(1, 1)
    gathered(1)
    y_stage(0, 2)
    y_stage(0, 0)
    wait_in(1)
    compute(1)

    def finish(i):
        q = partner_computes(i)
        cot = g_raw.at[i].reshape(2 * samples, LANES)
        target = blocks.at[q].reshape(2 * samples, LANES)

        def step(k, _):
            rows = [pl.multiple_of((k * UNROLL + u) * ROWS, ROWS) for u in range(UNROLL)]
            for u, row in enumerate(rows):
                at = pl.ds(row, ROWS)
                even, odd = halves(back[0, q, at, :].astype(F32), back[1, q, at, :].astype(F32))
                tmp[u, pl.ds(0, ROWS, stride=2), :] = even
                tmp[u, pl.ds(1, ROWS, stride=2), :] = odd
            for u, row in enumerate(rows):
                both = pl.ds(2 * row, 2 * ROWS)
                target[both, :] = (tmp[u] + cot[both, :].astype(F32)).astype(BF)
            return 0

        lax.fori_loop(0, samples // (ROWS * UNROLL), step, 0)

    def take_back(i):
        wait_for(back.at[:, 0], out_recv.at[inverse(i)])
        finish(i)

    wait_for(back.at[:, 0], own_out_sem)
    finish(0)
    for n in (2, 0, 1):
        relay_stage(n)
    y_stage(1, 2)
    for i in (2, 4, 6):
        take_back(i)
    y_stage(1, 0)
    x_stage(1, 2)
    take_back(1)
    y_stage(1, 1)
    x_stage(1, 0)
    take_back(7)
    x_stage(1, 1)
    take_back(5)
    for n in (2, 0, 1):
        last_stage(0, n)
    take_back(3)
    for n in (2, 0, 1):
        last_stage(1, n)

    for at in range(4):
        wait_shards(12, ag_send.at[at])
        wait_shards(9, ag_send.at[4 + at])
    wait_shards(24, rs1_send.at[1])
    for token in range(2):
        wait_shards(18, rs2_send.at[token])
        wait_for(stage.at[token, 0, pl.ds(1, TOKEN_DEVICES - 1)], out_send.at[token])
    wait_shards(6, rs3_send.at[0])
    wait_shards(3, rs3_send.at[1])

    @pl.when(xh == 0)
    def _():
        for at in (8, 9, 11, 13):
            wait_shards(3, ag_send.at[at])

    @pl.when(xh == 1)
    def _():
        for at in (10, 12, 14):
            wait_shards(3, ag_send.at[at])
        wait_shards(3, rs3_send.at[2])


def deliver(blocks, gate, up, down, out, out_gate, out_up, out_down, sem):
    copies = [
        pltpu.make_async_copy(
            blocks.at[q], out.at[:, :, pl.ds(q * LANES, LANES)], sem.at[q]
        )
        for q in range(TOKEN_DEVICES)
    ]
    pairs = ((gate, out_gate), (up, out_up), (down, out_down))
    copies += [pltpu.make_async_copy(a, b, sem.at[TOKEN_DEVICES + n]) for n, (a, b) in enumerate(pairs)]
    for copy in copies:
        copy.start()
    for copy in copies:
        copy.wait()


def solution(mesh):
    def per_device(inputs, cotangent, w_gate, w_up, w_down):
        samples, owned, width = inputs.shape
        up_rows, ff = w_gate.shape[1:]
        down_rows = w_down.shape[1]
        factor = float(samples * DP) ** -0.5
        anywhere = pl.BlockSpec(memory_space=pl.ANY)
        vmem = pl.BlockSpec(memory_space=pltpu.VMEM)
        dma = pltpu.SemaphoreType.DMA

        def three(*lead):
            return [
                pltpu.VMEM((*lead, up_rows, ff), BF),
                pltpu.VMEM((*lead, up_rows, ff), BF),
                pltpu.VMEM((*lead, down_rows, width), BF),
            ]

        raw = pltpu.VMEM((TOKEN_DEVICES, samples, owned, LANES), BF)
        hidden = pltpu.VMEM((samples, ff), BF)
        made = pl.pallas_call(
            functools.partial(kernel, factor),
            name="mixer_backward",
            out_shape=(
                raw,
                pltpu.VMEM(w_gate.shape, BF),
                pltpu.VMEM(w_up.shape, BF),
                pltpu.VMEM(w_down.shape, BF),
            ),
            in_specs=[anywhere] * 5,
            out_specs=(vmem,) * 4,
            scratch_shapes=[
                raw,
                pltpu.VMEM((2, 2, TOKEN_DEVICES, samples, LANES), BF),
                pltpu.VMEM((2, 2, samples, width), BF),
                *three(2, DP),
                hidden, hidden, hidden,
                pltpu.VMEM((UNROLL, 2 * ROWS, LANES), F32),
                *three(2, 4, 2),
                *three(2, 2, 4),
                *three(2, 3, 2),
                *three(2, 2),
                *three(2, 2),
                *three(),
                *three(),
                pltpu.VMEM((2, TOKEN_DEVICES, samples, LANES), BF),
                dma((TOKEN_DEVICES,)), dma(()), dma(()),
                dma((2,)), dma((2,)), dma((2,)), dma((TOKEN_DEVICES,)), dma(()),
                dma((15,)), dma((21,)),
                dma((2,)), dma((2, 3)), dma((2,)), dma((2, 3)), dma((3,)), dma((12,)),
            ],
            compiler_params=pltpu.CompilerParams(
                collective_id=0, has_side_effects=True, vmem_limit_bytes=62_000_000
            ),
        )(inputs, cotangent, w_gate, w_up, w_down)
        return pl.pallas_call(
            deliver,
            name="deliver",
            out_shape=(
                jax.ShapeDtypeStruct(inputs.shape, BF),
                jax.ShapeDtypeStruct(w_gate.shape, BF),
                jax.ShapeDtypeStruct(w_up.shape, BF),
                jax.ShapeDtypeStruct(w_down.shape, BF),
            ),
            in_specs=[vmem] * 4,
            out_specs=(anywhere,) * 4,
            scratch_shapes=[dma((TOKEN_DEVICES + 3,))],
            compiler_params=pltpu.CompilerParams(vmem_limit_bytes=1_000_000),
        )(*(pltpu.with_memory_space_constraint(a, pltpu.VMEM) for a in made))

    return jax.shard_map(
        per_device,
        mesh=mesh,
        in_specs=(
            P("dp", "token", None),
            P("dp", "token", None),
            P("token", "dp", None),
            P("token", "dp", None),
            P("token", "dp", None),
        ),
        out_specs=(
            P("dp", "token", None),
            P("token", "dp", None),
            P("token", "dp", None),
            P("token", "dp", None),
        ),
        check_vma=False,
    )
```
